32 devices in a mesh: dp: 8 (over y, x, core), tensor: 4 (over z).
Axes of the slice: x: 2, y: 2, z: 4, core: 2. Of those that a mesh axis runs over, the one named last changes fastest.
Arguments:
- acts: bfloat16 [8192, 256], P('dp'), may hold values from -6 to 6
- out_grad: bfloat16 [8192, 4096], P('dp', 'tensor'), may hold values from -6 to 6
- weight: float32 [256, 4096], P(None, 'tensor'), may hold values from -0.375 to 0.375
- error: float32 [8, 256, 4096], P('dp', None, 'tensor'), may hold values from -6 to 6
- start_q: float32 [4096, 64], P('tensor'), may hold values from -0.1875 to 0.1875
Outputs:
- new_weight: float32 [256, 4096], P(None, 'tensor')
- new_error: float32 [8, 256, 4096], P('dp', None, 'tensor')
- input_grad: float32 [8192, 256], P(('dp', 'tensor'))
The draws below stay inside these ranges and needn't reach their ends.
All inputs are finite; a program needn't handle non-finite values.
Results may differ from the reference program's by a relative error of at most 0.0003.
Values sent between devices are 32-bit elements; how exact they have to be, the bound alone decides.
No kernel may reach another device: no remote copies, remote signals or barrier semaphores. Data moves between devices by JAX's collectives and lax.ppermute only.
A program may use at most 64 MiB of HBM per device.

```python
import math
import jax
import jax.numpy as jnp
from jax import lax

DIN = 256
COL_DEV = 1024
RANK = 64
TOK_DEV = 1024
COLS = 4096
TOKENS = 8192
REPLICAS = 8
N_TENSOR = 4


def block_scale(key, dims, shards, least, top_value):
    def one(axis_at, parts):
        heights = jax.random.uniform(jax.random.fold_in(jax.random.fold_in(key, 6), axis_at), (parts,), jnp.float32, least / len(shards), top_value / len(shards))
        return jnp.repeat(jnp.exp(heights), dims[axis_at] // parts).reshape((-1,) + (1,) * (len(dims) - axis_at - 1))

    loudness = one(*shards[0])
    for cut in shards[1:]:
        loudness = loudness * one(*cut)
    return loudness


def gaussian(own_key, dims, width, bound, cuts=(), kind=jnp.bfloat16):
    drawn = width * jax.random.normal(own_key, dims, jnp.float32)
    if cuts:
        drawn = drawn * block_scale(own_key, dims, cuts, -0.22, 0.18)
    return jnp.clip(drawn, -bound, bound).astype(kind)


def setup_inputs(seed: int = 0) -> dict:
    key_list = jax.random.split(jax.random.key(seed), 6)
    acts = gaussian(key_list[0], (TOKENS, DIN), 1.0, 6.0, ((0, 8),))
    out_grad = gaussian(key_list[1], (TOKENS, COLS), 1.0, 6.0, ((0, 8), (1, 4)))
    weight = gaussian(key_list[2], (DIN, COLS), DIN ** -0.5, 0.375, ((1, 4),), jnp.float32)
    error = gaussian(key_list[3], (REPLICAS, DIN, COLS), 1.0, 6.0, ((0, 8), (2, 4)), jnp.float32)
    start_q = gaussian(key_list[4], (COLS, RANK), COL_DEV ** -0.5, 0.1875, ((0, 4),), jnp.float32)
    return dict(acts=acts, out_grad=out_grad, weight=weight, error=error, start_q=start_q)


HIGH = lax.Precision.HIGHEST

def one_tile(carry, pieces):
    acts32, grads_t, error_t, weight_t, start_t = pieces
    grads32 = grads_t.astype(jnp.float32)
    gradient = jnp.einsum('rtd,rtc->rdc', acts32, grads32, precision=HIGH) / math.sqrt(TOK_DEV)
    merged = gradient + error_t
    left = lax.optimization_barrier(jnp.sum(jnp.einsum('rdc,ck->rdk', merged, start_t, precision=HIGH), axis=0)) / REPLICAS
    gram = jnp.dot(left.T, left, precision=HIGH)
    chol = jnp.linalg.cholesky(gram)
    ortho = jax.scipy.linalg.solve_triangular(chol, left.T, lower=True).T
    right = lax.optimization_barrier(jnp.sum(jnp.einsum('rdc,dk->rck', merged, ortho, precision=HIGH), axis=0)) / REPLICAS
    delta = jnp.dot(ortho, right.T, precision=HIGH)
    part = jnp.einsum('rtc,dc->rtd', grads32, weight_t, precision=HIGH)
    return (carry + part, (merged - delta[None], weight_t - delta))

def reference(acts, out_grad, weight, error, start_q):
    acts32 = acts.astype(jnp.float32).reshape(REPLICAS, TOK_DEV, DIN)
    grads = out_grad.reshape(REPLICAS, TOK_DEV, N_TENSOR, COL_DEV).transpose(2, 0, 1, 3)
    errors = error.reshape(REPLICAS, DIN, N_TENSOR, COL_DEV).transpose(2, 0, 1, 3)
    weights = weight.reshape(DIN, N_TENSOR, COL_DEV).transpose(1, 0, 2)
    starts = start_q.reshape(N_TENSOR, COL_DEV, RANK)
    init = jnp.zeros((REPLICAS, TOK_DEV, DIN), jnp.float32)

    def stepper(carry, items):
        return one_tile(carry, (acts32,) + items)
    total, outs = lax.scan(stepper, init, (grads, errors, weights, starts))
    new_errors, new_weights = outs
    new_error = new_errors.transpose(1, 2, 0, 3).reshape(REPLICAS, DIN, COLS)
    new_weight = new_weights.transpose(1, 0, 2).reshape(DIN, COLS)
    return (new_weight, new_error, total.reshape(TOKENS, DIN))
```

```python
import math

import jax
import jax.numpy as jnp
from jax import lax
from jax.sharding import PartitionSpec as P

HIGH = lax.Precision.HIGH


def flip(bit_even, bit_odd, size):
    return [(i, i ^ (bit_odd if i & 1 else bit_even)) for i in range(size)]


def local(acts, out_grad, weight, error, start_q):
    tok_rows = acts.shape[0]
    din, cols = weight.shape
    replicas = lax.axis_size("dp")
    n_tensor = lax.axis_size("tensor")
    half = cols // 2
    side = lax.axis_index("dp") % 2
    t_idx = lax.axis_index("tensor")
    bits = [1 << b for b in range(1, replicas.bit_length() - 1)]

    gradient = jnp.einsum(
        "td,tc->dc", acts, out_grad, preferred_element_type=jnp.float32
    ) / math.sqrt(tok_rows)
    merged = gradient + error[0]
    left = lax.dot_general(start_q, merged, (((0,), (1,)), ((), ())), precision=HIGH)

    mine = lax.dynamic_slice(merged, (0, side * half), (din, half))
    theirs = lax.dynamic_slice(merged, (0, (1 - side) * half), (din, half))
    pair = flip(1, 1, replicas)
    left = left + lax.ppermute(left, "dp", pair)
    total = mine + lax.ppermute(theirs, "dp", pair)

    partial_sum = jnp.dot(out_grad.astype(jnp.float32), weight.T, precision=HIGH)
    block = tok_rows // n_tensor

    def rows(k):
        return lax.dynamic_slice(partial_sum, (((t_idx + k) % n_tensor) * block, 0), (block, din))

    input_grad = rows(0)
    for k in range(1, n_tensor):
        input_grad = input_grad + lax.ppermute(
            rows(k), "tensor", [(i, (i + k) % n_tensor) for i in range(n_tensor)]
        )

    for even, odd in zip(bits, bits[::-1]):
        swap = flip(even, odd, replicas)
        left = left + lax.ppermute(left, "dp", flip(even, even, replicas))
        total = total + lax.ppermute(total, "dp", swap)
    left = left / replicas
    gram = lax.dot_general(left, left, (((1,), (1,)), ((), ())), precision=lax.Precision.HIGHEST)
    chol = jnp.linalg.cholesky(gram)
    ortho = jax.scipy.linalg.solve_triangular(chol, left, lower=True)
    right = jnp.dot(ortho, total, precision=HIGH) / replicas
    other = lax.ppermute(right, "dp", pair)
    right = jnp.where(side == 0, jnp.concatenate([right, other], 1), jnp.concatenate([other, right], 1))
    delta = lax.dot_general(ortho, right, (((0,), (0,)), ((), ())), precision=HIGH)
    return (weight - delta, (merged - delta)[None], input_grad)


def solution(mesh):
    placed = (
        P("dp", None),
        P("dp", "tensor"),
        P(None, "tensor"),
        P("dp", None, "tensor"),
        P("tensor", None),
    )
    return jax.shard_map(
        local,
        mesh=mesh,
        in_specs=placed,
        out_specs=(P(None, "tensor"), P("dp", None, "tensor"), P(("dp", "tensor"), None)),
        check_vma=False,
    )
```

```python
import functools
import math

import jax
import jax.numpy as jnp
from jax import lax
from jax.experimental import pallas as pl
from jax.experimental.pallas import tpu as pltpu
from jax.sharding import PartitionSpec as P

F32 = jnp.float32
BF16 = jnp.bfloat16
NN = (((1,), (0,)), ((), ()))
NT = (((1,), (1,)), ((), ()))
VMEM = pl.BlockSpec(memory_space=pltpu.VMEM)
ANY = pl.BlockSpec(memory_space=pl.ANY)
HBM = pl.BlockSpec(memory_space=pltpu.HBM)


def swap(bit_even, bit_odd, size):
    return [(i, i ^ (bit_odd if i & 1 else bit_even)) for i in range(size)]


def split(x):
    high = x.astype(BF16)
    return high, (x - high.astype(F32)).astype(BF16)


def dot(a, b, dims):
    return lax.dot_general(a, b, dims, preferred_element_type=F32)


def dot3(a, b, dims):
    (ah, al), (bh, bl) = split(a), split(b)
    return dot(ah, bh, dims) + (dot(ah, bl, dims) + dot(al, bh, dims))


def front_kernel(chunks, n_tensor, acts, og, wt, err, qt, *rest):
    theirs, mine, left = rest[:3]
    blocks = rest[3 : 3 + n_tensor]
    acts_v, og_v, wt_v, err_v, qt_v, acts_t, part, sems = rest[3 + n_tensor :]
    tok, din = acts.shape
    cols = og.shape[1]
    width = cols // chunks
    half = chunks // 2
    side = lax.rem(lax.axis_index("dp"), 2)
    copies = [pltpu.make_async_copy(acts, acts_v, sems.at[4 * chunks])]
    copies[0].start()
    for c in range(chunks):
        at = pl.multiple_of(lax.rem((1 - side) * half + c, chunks) * width, width)
        span = pl.ds(at, width)
        group = [
            pltpu.make_async_copy(og.at[:, span], og_v.at[c], sems.at[4 * c]),
            pltpu.make_async_copy(err.at[0, :, span], err_v.at[c], sems.at[4 * c + 1]),
            pltpu.make_async_copy(qt.at[:, span], qt_v.at[c], sems.at[4 * c + 2]),
            pltpu.make_async_copy(wt.at[:, span], wt_v.at[c], sems.at[4 * c + 3]),
        ]
        for one in group:
            one.start()
        copies.append(group)
    copies[0].wait()
    acts_t[...] = acts_v[...].T
    scale = 1.0 / math.sqrt(tok)
    for c in range(chunks):
        group = copies[1 + c]
        group[0].wait()
        grad = dot(acts_t[...], og_v[c], NN)
        group[1].wait()
        merged = grad * scale + err_v[c]
        out = theirs if c < half else mine
        out[:, (c % half) * width : (c % half + 1) * width] = merged
        group[2].wait()
        add = dot3(qt_v[c], merged, NT)
        if c == 0:
            left[...] = add
        else:
            left[...] += add
        group[3].wait()
        high, low = split(wt_v[c])
        add = dot(og_v[c], high, NT) + dot(og_v[c], low, NT)
        if c == 0:
            part[...] = add
        elif c < chunks - 1:
            part[...] += add
        else:
            part[...] += add
    me = lax.axis_index("tensor")
    block = tok // n_tensor
    for k in range(n_tensor):
        at = pl.multiple_of(lax.rem(me + k, n_tensor) * block, block)
        blocks[k][...] = part[pl.ds(at, block), :]


def front(acts, og, wt, err, qt, n_tensor):
    tok, din = acts.shape
    cols = og.shape[1]
    rank = qt.shape[0]
    chunks = 4 if cols % 512 == 0 else 2
    width = cols // chunks
    shape = jax.ShapeDtypeStruct
    return pl.pallas_call(
        functools.partial(front_kernel, chunks, n_tensor),
        out_shape=[shape((din, cols // 2), F32)] * 2
        + [shape((rank, din), F32)]
        + [shape((tok // n_tensor, din), F32)] * n_tensor,
        in_specs=[HBM] * 5,
        out_specs=[VMEM] * (3 + n_tensor),
        scratch_shapes=[
            pltpu.VMEM((tok, din), BF16),
            pltpu.VMEM((chunks, tok, width), BF16),
            pltpu.VMEM((chunks, din, width), F32),
            pltpu.VMEM((chunks, din, width), F32),
            pltpu.VMEM((chunks, rank, width), F32),
            pltpu.VMEM((din, tok), BF16),
            pltpu.VMEM((tok, din), F32),
            pltpu.SemaphoreType.DMA((4 * chunks + 1,)),
        ],
        compiler_params=pltpu.CompilerParams(vmem_limit_bytes=24 << 20),
        cost_estimate=pl.CostEstimate(
            flops=6 * tok * din * cols, bytes_accessed=5 << 20, transcendentals=0
        ),
        name="front",
    )(acts, og, wt, err, qt)


def ortho_kernel(replicas, a_ref, b_ref, o_ref):
    left = (a_ref[...] + b_ref[...]) * (1.0 / replicas)
    rank, din = left.shape
    gram = lax.dot_general(
        left, left, NT, precision=lax.Precision.HIGHEST, preferred_element_type=F32
    )
    tiles = rank // 8
    gs = [gram[8 * i : 8 * i + 8, :] for i in range(tiles)]
    ls = [left[8 * i : 8 * i + 8, :] for i in range(tiles)]
    for k in range(rank):
        i, s = divmod(k, 8)
        columns = [jnp.broadcast_to(g[:, k : k + 1], (8, din)) for g in gs[i:]]
        pivot = columns[0][s : s + 1, :]
        inverse = 1.0 / pivot
        row_g = gs[i][s : s + 1, :]
        row_l = ls[i][s : s + 1, :]
        o_ref[k : k + 1, :] = row_l * lax.rsqrt(pivot)
        if k == rank - 1:
            break
        step_g = row_g * inverse[:, :rank]
        step_l = row_l * inverse
        for j in range(i, tiles):
            gs[j] = gs[j] - columns[j - i][:, :rank] * step_g
            ls[j] = ls[j] - columns[j - i] * step_l


def ortho_of(a, b, replicas):
    rank, din = a.shape
    return pl.pallas_call(
        functools.partial(ortho_kernel, replicas),
        out_shape=jax.ShapeDtypeStruct((rank, din), F32),
        in_specs=[VMEM] * 2,
        out_specs=VMEM,
        compiler_params=pltpu.CompilerParams(vmem_limit_bytes=4 << 20),
        cost_estimate=pl.CostEstimate(
            flops=1 << 30, bytes_accessed=1 << 20, transcendentals=0
        ),
        name="ortho",
    )(a, b)


def right_kernel(replicas, o_ref, a_ref, b_ref, r_ref):
    r_ref[...] = dot3(o_ref[...], a_ref[...] + b_ref[...], NN) * (1.0 / replicas)


def right_of(ortho, a, b, replicas):
    return pl.pallas_call(
        functools.partial(right_kernel, replicas),
        out_shape=jax.ShapeDtypeStruct((ortho.shape[0], a.shape[1]), F32),
        in_specs=[VMEM] * 3,
        out_specs=VMEM,
        compiler_params=pltpu.CompilerParams(vmem_limit_bytes=8 << 20),
        name="right",
    )(ortho, a, b)


def back_kernel(chunks, o_ref, mine_r, theirs_r, mine, theirs, wt, new_w, new_e, wv, ev, sems):
    cols = wt.shape[1]
    width = cols // chunks
    half = chunks // 2
    side = lax.rem(lax.axis_index("dp"), 2)
    flipped = o_ref[...].T
    copies = []
    for c in range(chunks):
        at = pl.multiple_of(lax.rem(side * half + c, chunks) * width, width)
        here = slice((c % half) * width, (c % half + 1) * width)
        right, merged = (mine_r, mine) if c < half else (theirs_r, theirs)
        delta = dot3(flipped, right[:, here], NN)
        ev[c] = merged[:, here] - delta
        wv[c] = wt[:, pl.ds(at, width)] - delta
        for one in (
            pltpu.make_async_copy(ev.at[c], new_e.at[0, :, pl.ds(at, width)], sems.at[2 * c]),
            pltpu.make_async_copy(wv.at[c], new_w.at[:, pl.ds(at, width)], sems.at[2 * c + 1]),
        ):
            one.start()
            copies.append(one)
    for one in copies:
        one.wait()


def back(ortho, mine_r, theirs_r, mine, theirs, wt):
    din, cols = wt.shape
    chunks = 4 if cols % 512 == 0 else 2
    width = cols // chunks
    return pl.pallas_call(
        functools.partial(back_kernel, chunks),
        out_shape=[
            jax.ShapeDtypeStruct((din, cols), F32),
            jax.ShapeDtypeStruct((1, din, cols), F32),
        ],
        in_specs=[VMEM] * 6,
        out_specs=[ANY] * 2,
        scratch_shapes=[
            pltpu.VMEM((chunks, din, width), F32),
            pltpu.VMEM((chunks, din, width), F32),
            pltpu.SemaphoreType.DMA((2 * chunks,)),
        ],
        compiler_params=pltpu.CompilerParams(vmem_limit_bytes=16 << 20),
        name="back",
    )(ortho, mine_r, theirs_r, mine, theirs, wt)


def local(acts, out_grad, weight, error, start_q):
    replicas = lax.axis_size("dp")
    n_tensor = lax.axis_size("tensor")
    bits = [1 << b for b in range(1, replicas.bit_length() - 1)]
    pair = swap(1, 1, replicas)

    theirs, mine, left, *blocks = front(
        acts, out_grad, weight, error, start_q.T, n_tensor
    )
    total = mine + lax.ppermute(theirs, "dp", pair)
    left = left + lax.ppermute(left, "dp", pair)
    input_grad = blocks[0]
    for k in range(1, n_tensor):
        hop = [(i, (i + k) % n_tensor) for i in range(n_tensor)]
        input_grad = input_grad + lax.ppermute(blocks[k], "tensor", hop)

    for even, odd in zip(bits[:-1], bits[:0:-1]):
        total = total + lax.ppermute(total, "dp", swap(even, odd, replicas))
        left = left + lax.ppermute(left, "dp", swap(even, even, replicas))
    last_total = lax.ppermute(total, "dp", swap(bits[-1], bits[0], replicas))
    last_left = lax.ppermute(left, "dp", swap(bits[-1], bits[-1], replicas))
    ortho = ortho_of(left, last_left, replicas)
    right = right_of(ortho, total, last_total, replicas)
    other = lax.ppermute(right, "dp", pair)
    new_weight, new_error = back(ortho, right, other, mine, theirs, weight)
    return (new_weight, new_error, input_grad)


def solution(mesh):
    placed = (
        P("dp", None),
        P("dp", "tensor"),
        P(None, "tensor"),
        P("dp", None, "tensor"),
        P("tensor", None),
    )
    return jax.shard_map(
        local,
        mesh=mesh,
        in_specs=placed,
        out_specs=(P(None, "tensor"), P("dp", None, "tensor"), P(("dp", "tensor"), None)),
        check_vma=False,
    )
```

```python
import functools
import math

import jax
import jax.numpy as jnp
from jax import lax
from jax.experimental import pallas as pl
from jax.experimental.pallas import tpu as pltpu
from jax.sharding import PartitionSpec as P


F32 = jnp.float32
BF16 = jnp.bfloat16
NN = (((1,), (0,)), ((), ()))
NT = (((1,), (1,)), ((), ()))
VMEM_BYTES = 67043328
SPARE = 13 << 20
VMEM = pl.BlockSpec(memory_space=pltpu.VMEM)
ANY = pl.BlockSpec(memory_space=pl.ANY)
HBM = pl.BlockSpec(memory_space=pltpu.HBM)


def swap(bit_even, bit_odd, size):
    return [(i, i ^ (bit_odd if i & 1 else bit_even)) for i in range(size)]


def split(x):
    high = x.astype(BF16)
    return high, (x - high.astype(F32)).astype(BF16)


def dot(a, b, dims):
    return lax.dot_general(a, b, dims, preferred_element_type=F32)


def dot3(a, b, dims):
    (ah, al), (bh, bl) = split(a), split(b)
    return dot(ah, bh, dims) + (dot(ah, bl, dims) + dot(al, bh, dims))


def grad_kernel(chunks, acts, og, err, theirs, mine, *rest):
    og_v = rest[:chunks]
    acts_v, err_v, acts_t, sems = rest[chunks:]
    tok, _ = acts.shape
    cols = og.shape[1]
    width = cols // chunks
    half = chunks // 2
    side = lax.rem(lax.axis_index("dp"), 2)
    first = pltpu.make_async_copy(acts, acts_v, sems.at[chunks])
    first.start()
    halves = []
    for n, where in enumerate((1 - side, side)):
        loads = []
        for c in range(n * half, (n + 1) * half):
            at = pl.multiple_of((where * half + c - n * half) * width, width)
            loads.append(pltpu.make_async_copy(og.at[:, pl.ds(at, width)], og_v[c], sems.at[c]))
        at = pl.multiple_of(where * half * width, half * width)
        err_part = err.at[0, :, pl.ds(at, half * width)]
        loads.append(pltpu.make_async_copy(err_part, err_v.at[n], sems.at[chunks + 1 + n]))
        for load in loads:
            load.start()
        halves.append(loads)
    first.wait()
    acts_t[...] = acts_v[...].T
    scale = 1.0 / math.sqrt(tok)
    for n, out in enumerate((theirs, mine)):
        for load in halves[n]:
            load.wait()
        columns = [og_v[c][...] for c in range(n * half, (n + 1) * half)]
        grad = dot(acts_t[...], jnp.concatenate(columns, axis=1), NN)
        out[...] = grad * scale + err_v[n]


def merged_of(acts, og, err):
    tok, din = acts.shape
    cols = og.shape[1]
    chunks = 4
    shape = jax.ShapeDtypeStruct
    return pl.pallas_call(
        functools.partial(grad_kernel, chunks),
        out_shape=[shape((din, cols // 2), F32)] * 2
        + [shape((tok, cols // chunks), BF16)] * chunks,
        in_specs=[HBM] * 3,
        out_specs=[VMEM] * (2 + chunks),
        scratch_shapes=[
            pltpu.VMEM((tok, din), BF16),
            pltpu.VMEM((2, din, cols // 2), F32),
            pltpu.VMEM((din, tok), BF16),
            pltpu.SemaphoreType.DMA((chunks + 3,)),
        ],
        compiler_params=pltpu.CompilerParams(vmem_limit_bytes=VMEM_BYTES - SPARE),
        cost_estimate=pl.CostEstimate(
            flops=2 * tok * din * cols, bytes_accessed=4 << 20, transcendentals=0
        ),
        name="merged",
    )(acts, og, err)


def rounds_of(n):
    flows = [(a, b) for a in range(n) for b in range(n) if a != b]
    relay, last = {}, {}
    if n >= 4:
        relay = {0: (1, n - 1), n - 1: (n - 2, 0), 1: (0, 0), n - 2: (n - 1, n - 1)}
        last = {1: (n - 1, n - 1), n - 2: (0, 0)}
        gone = [(0, n - 1), (n - 1, 0), (1, 0), (n - 2, n - 1), (1, n - 1), (n - 2, 0)]
        flows = [flow for flow in flows if flow not in gone]
    flows.sort(key=lambda flow: (abs(flow[0] - flow[1]), flow))

    def fill(chosen):
        for a, b in list(flows):
            if a not in chosen and all(b != to for to, _ in chosen.values()):
                chosen[a] = (b, b)
                flows.remove((a, b))
        return chosen

    fill(last)
    plain = []
    while flows:
        plain.append(fill({}))
    return relay, plain, last


def pick(me, table, n):
    index = jnp.int32(0)
    for a in range(n):
        index = jnp.where(me == a, table[a][1] if a in table else a, index)
    return index


def part_kernel(tables, n_tensor, chunks, wt, *rest):
    og, blocks, wt_2 = rest[:chunks], rest[chunks:-1], rest[-1]
    cols = wt.shape[1]
    tok, width = og[0].shape
    side = lax.rem(lax.axis_index("dp"), 2)
    for c in range(chunks):
        at = pl.multiple_of(lax.rem((1 - side) * (chunks // 2) + c, chunks) * width, width)
        high, low = split(wt[:, pl.ds(at, width)])
        wt_2[:, c * width : (c + 1) * width] = high
        wt_2[:, cols + c * width : cols + (c + 1) * width] = low
    me = lax.axis_index("tensor")
    block = tok // n_tensor
    for table, out in zip(tables, blocks):
        at = pl.multiple_of(pick(me, table, n_tensor) * block, block)
        rows = [one[pl.ds(at, block), :] for one in og]
        out[...] = dot(jnp.concatenate(rows + rows, axis=1), wt_2[...], NT)


def parts_of(og, wt, n_tensor, tables):
    tok = og[0].shape[0]
    din, cols = wt.shape
    count = len(tables)
    return pl.pallas_call(
        functools.partial(part_kernel, tables, n_tensor, len(og)),
        out_shape=[jax.ShapeDtypeStruct((tok // n_tensor, din), F32)] * count,
        in_specs=[VMEM] * (1 + len(og)),
        out_specs=[VMEM] * count,
        scratch_shapes=[pltpu.VMEM((din, 2 * cols), BF16)],
        compiler_params=pltpu.CompilerParams(vmem_limit_bytes=16 << 20),
        cost_estimate=pl.CostEstimate(
            flops=4 * tok * din * cols, bytes_accessed=4 << 20, transcendentals=0
        ),
        name="part",
    )(wt, *og)


def is_between(n_tensor):
    me = lax.axis_index("tensor")
    return ((me == 1) | (me == n_tensor - 2)).astype(F32)


def onward_kernel(n_tensor, block, relayed, out):
    out[...] = block[...] + is_between(n_tensor) * relayed[...]


def gather_kernel(n_tensor, relayed, own, *rest):
    total = own[...]
    if relayed is not None:
        total = total + (1.0 - is_between(n_tensor)) * relayed[...]
    for part in rest[:-1]:
        total = total + part[...]
    rest[-1][...] = total


def summed(kernel, *parts):
    return pl.pallas_call(
        kernel,
        out_shape=jax.ShapeDtypeStruct(parts[0].shape, F32),
        in_specs=[VMEM] * len(parts),
        out_specs=VMEM,
        compiler_params=pltpu.CompilerParams(vmem_limit_bytes=4 << 20),
    )(*parts)


def left_kernel(qt, theirs, mine, o_ref):
    half = theirs.shape[1]
    side = lax.rem(lax.axis_index("dp"), 2)
    far = qt[:, pl.ds(pl.multiple_of((1 - side) * half, half), half)]
    near = qt[:, pl.ds(pl.multiple_of(side * half, half), half)]
    o_ref[...] = dot3(far, theirs[...], NT) + dot3(near, mine[...], NT)


def left_of(qt, theirs, mine):
    return pl.pallas_call(
        left_kernel,
        out_shape=jax.ShapeDtypeStruct((qt.shape[0], mine.shape[0]), F32),
        in_specs=[VMEM] * 3,
        out_specs=VMEM,
        compiler_params=pltpu.CompilerParams(vmem_limit_bytes=8 << 20),
        name="left",
    )(qt, theirs, mine)


def solve_kernel(replicas, a_ref, b_ref, y_ref):
    left = (a_ref[...] + b_ref[...]) * (1.0 / replicas)
    rank, din = left.shape
    gram = lax.dot_general(
        left, left, NT, precision=lax.Precision.HIGHEST, preferred_element_type=F32
    )
    tiles, lanes = rank // 8, 128
    spans = range(0, din, lanes)
    state = [
        [gram[8 * i : 8 * i + 8, :]] + [left[8 * i : 8 * i + 8, at : at + lanes] for at in spans]
        for i in range(tiles)
    ]
    sub = lax.broadcasted_iota(jnp.int32, (8, lanes), 0)
    for k in range(0, rank, 2):
        i, s = divmod(k, 8)
        first = [jnp.broadcast_to(row[0][:, k : k + 1], (8, lanes)) for row in state]
        second = [jnp.broadcast_to(row[0][:, k + 1 : k + 2], (8, lanes)) for row in state]
        a = first[i][s : s + 1, :]
        b = second[i][s : s + 1, :]
        d = second[i][s + 1 : s + 2, :]
        inverse = 1.0 / (a * d - b * b)
        p, q, r = d * inverse, b * inverse, a * inverse
        for part in range(len(state[0])):
            wide = state[0][part].shape[1]
            top = state[i][part][s : s + 1, :]
            low = state[i][part][s + 1 : s + 2, :]
            new_top = p[:, :wide] * top - q[:, :wide] * low
            new_low = r[:, :wide] * low - q[:, :wide] * top
            for j in range(tiles):
                old = state[j][part]
                new = old - first[j][:, :wide] * new_top - second[j][:, :wide] * new_low
                if j == i:
                    new = jnp.where(sub[:, :wide] == s, new_top, new)
                    new = jnp.where(sub[:, :wide] == s + 1, new_low, new)
                state[j][part] = new
    for j in range(tiles):
        for n, at in enumerate(spans):
            y_ref[8 * j : 8 * j + 8, at : at + lanes] = state[j][1 + n]


def solve(a, b, replicas):
    return pl.pallas_call(
        functools.partial(solve_kernel, replicas),
        out_shape=jax.ShapeDtypeStruct(a.shape, F32),
        in_specs=[VMEM] * 2,
        out_specs=VMEM,
        compiler_params=pltpu.CompilerParams(vmem_limit_bytes=4 << 20),
        cost_estimate=pl.CostEstimate(
            flops=1 << 30, bytes_accessed=1 << 20, transcendentals=0
        ),
        name="solve",
    )(a, b)


def begin_kernel(mine, came, *out):
    width = out[0].shape[1]
    for n, ref in enumerate(out):
        here = slice(n * width, (n + 1) * width)
        ref[...] = mine[:, here] + came[:, here]


def begin(mine, came):
    din, half = mine.shape
    return pl.pallas_call(
        begin_kernel,
        out_shape=[jax.ShapeDtypeStruct((din, half // 2), F32)] * 2,
        in_specs=[VMEM] * 2,
        out_specs=[VMEM] * 2,
        compiler_params=pltpu.CompilerParams(vmem_limit_bytes=4 << 20),
        name="begin",
    )(mine, came)


def right_kernel(replicas, left_a, left_b, *rest):
    out = rest[-1]
    left = (left_a[...] + left_b[...]) * (1.0 / replicas)
    width = rest[0].shape[1]
    for n in range(2):
        total = (rest[2 * n][...] + rest[2 * n + 1][...]) * (1.0 / replicas)
        out[:, n * width : (n + 1) * width] = dot3(left, total, NN)


def right_of(left, left_came, parts, replicas):
    width = parts[0].shape[1]
    return pl.pallas_call(
        functools.partial(right_kernel, replicas),
        out_shape=jax.ShapeDtypeStruct((left.shape[0], 2 * width), F32),
        in_specs=[VMEM] * 6,
        out_specs=VMEM,
        compiler_params=pltpu.CompilerParams(vmem_limit_bytes=8 << 20),
        name="right",
    )(left, left_came, *parts)


def back_kernel(near, chunks, o_ref, right, merged, wt, *rest):
    new_w, new_e, wv, ev, sems = rest[-5:]
    width = merged.shape[1] // chunks
    side = lax.rem(lax.axis_index("dp"), 2)
    base = (side if near else 1 - side) * chunks
    flipped = o_ref[...].T
    copies = []
    for c in range(chunks):
        span = pl.ds(pl.multiple_of((base + c) * width, width), width)
        here = slice(c * width, (c + 1) * width)
        delta = dot3(flipped, right[:, here], NN)
        ev[c] = merged[:, here] - delta
        wv[c] = wt[:, span] - delta
        for one in (
            pltpu.make_async_copy(ev.at[c], new_e.at[0, :, span], sems.at[2 * c]),
            pltpu.make_async_copy(wv.at[c], new_w.at[:, span], sems.at[2 * c + 1]),
        ):
            one.start()
            copies.append(one)
    for one in copies:
        one.wait()


def back(near, ortho, right, merged, wt, *kept):
    din, cols = wt.shape
    chunks = 2
    width = cols // 2 // chunks
    return pl.pallas_call(
        functools.partial(back_kernel, near, chunks),
        out_shape=[
            jax.ShapeDtypeStruct((din, cols), F32),
            jax.ShapeDtypeStruct((1, din, cols), F32),
        ],
        in_specs=[VMEM] * 4 + [ANY] * len(kept),
        out_specs=[ANY] * 2,
        input_output_aliases={4 + n: n for n in range(len(kept))},
        scratch_shapes=[
            pltpu.VMEM((chunks, din, width), F32),
            pltpu.VMEM((chunks, din, width), F32),
            pltpu.SemaphoreType.DMA((2 * chunks,)),
        ],
        compiler_params=pltpu.CompilerParams(vmem_limit_bytes=16 << 20),
        name="back_near" if near else "back_far",
    )(ortho, right, merged, wt, *kept)


def send(x, axis, pairs):
    return lax.ppermute(x, axis, pairs)


def step(acts, out_grad, weight, error, start_q):
    replicas = lax.axis_size("dp")
    n_tensor = lax.axis_size("tensor")
    bits = [1 << b for b in range(1, replicas.bit_length() - 1)]
    pair = swap(1, 1, replicas)

    theirs, mine, *out_grad = merged_of(acts, out_grad, error)
    came = send(theirs, "dp", pair)
    left = left_of(start_q.T, theirs, mine)
    left_came = send(left, "dp", pair)
    relay, plain, last = rounds_of(n_tensor)
    shared = []
    for table in plain:
        fits = [held for held in shared if not held.keys() & table.keys()]
        if fits:
            fits[0].update(table)
        else:
            shared.append(dict(table))
    tables = shared + [{}] + ([relay, last] if relay else [])
    blocks = parts_of(out_grad, weight, n_tensor, tables)
    totals = begin(mine, came)
    comes = [None, None]
    for n, (one, other) in enumerate(zip(bits, bits[::-1]), 1):
        if n > 1:
            totals = [total + came for total, came in zip(totals, comes)]
        left = left + left_came
        left_came = send(left, "dp", swap(one, one, replicas))
        comes = [
            send(total, "dp", swap(bit, bit, replicas))
            for total, bit in zip(totals, (one, other))
        ]

    def pass_on(block, table):
        return send(block, "tensor", [(a, to) for a, (to, _) in sorted(table.items())])

    received = []
    for table in plain:
        held = next(at for at, one in enumerate(shared) if table.items() <= one.items())
        received.append(pass_on(blocks[held], table))
    own = blocks[len(shared)]
    if relay:
        relayed = pass_on(blocks[-2], relay)
        onward = summed(functools.partial(onward_kernel, n_tensor), blocks[-1], relayed)
        received.append(pass_on(onward, last))
        gather = functools.partial(gather_kernel, n_tensor)
        received = [relayed, own, *received]
    else:
        gather = functools.partial(gather_kernel, n_tensor, None)
        received = [own, *received]
    input_grad = summed(gather, *received)

    basis = solve(left, left_came, replicas)
    parts = [totals[0], comes[0], totals[1], comes[1]]
    right = right_of(left, left_came, parts, replicas)
    other = send(right, "dp", pair)
    kept = back(True, basis, right, mine, weight)
    new_weight, new_error = back(False, basis, other, theirs, weight, *kept)
    return (new_weight, new_error, input_grad)


def solution(mesh):
    placed = (
        P("dp", None),
        P("dp", "tensor"),
        P(None, "tensor"),
        P("dp", None, "tensor"),
        P("tensor", None),
    )
    return jax.shard_map(
        step,
        mesh=mesh,
        in_specs=placed,
        out_specs=(P(None, "tensor"), P("dp", None, "tensor"), P(("dp", "tensor"), None)),
        check_vma=False,
    )
```

```python
import functools
import math

import jax
import jax.numpy as jnp
from jax import lax
from jax.experimental import pallas as pl
from jax.experimental.pallas import tpu as pltpu
from jax.sharding import PartitionSpec as P


F32 = jnp.float32
BF16 = jnp.bfloat16
NN = (((1,), (0,)), ((), ()))
NT = (((1,), (1,)), ((), ()))
VMEM_BYTES = 67043328
SPARE = 27 << 19
VMEM = pl.BlockSpec(memory_space=pltpu.VMEM)
ANY = pl.BlockSpec(memory_space=pl.ANY)
HBM = pl.BlockSpec(memory_space=pltpu.HBM)


def swap(bit_even, bit_odd, size):
    return [(i, i ^ (bit_odd if i & 1 else bit_even)) for i in range(size)]


def split(x):
    high = x.astype(BF16)
    return high, (x - high.astype(F32)).astype(BF16)


def dot(a, b, dims):
    return lax.dot_general(a, b, dims, preferred_element_type=F32)


def dot3(a, b, dims):
    (ah, al), (bh, bl) = split(a), split(b)
    return dot(ah, bh, dims) + (dot(ah, bl, dims) + dot(al, bh, dims))


def rounds_of(n):
    flows = sorted(
        ((a, b) for a in range(n) for b in range(n) if a != b),
        key=lambda flow: (abs(flow[0] - flow[1]), flow),
    )

    def fill(chosen, order):
        for a, b in list(flows)[::order]:
            if a not in chosen and all(b != to for to, _ in chosen.values()):
                chosen[a] = (b, b)
                flows.remove((a, b))
        return chosen

    relay, last = {}, {}
    if n >= 4:
        for gone in ((0, n - 2), (n - 1, 1), (1, n - 2), (n - 2, 1)):
            flows.remove(gone)
        relay = fill({0: (1, n - 2), n - 1: (n - 2, 1)}, -1)
        last = fill({1: (n - 2, n - 2), n - 2: (1, 1)}, -1)
    plain = []
    while flows:
        plain.append(fill({}, 1))
    rounds = [relay, last, *plain] if relay else plain
    if len(rounds) == n - 1 and all(len(one) == n for one in rounds):
        return rounds, bool(relay)
    return [{a: ((a + k) % n,) * 2 for a in range(n)} for k in range(1, n)], False


def pick(me, table, n):
    index = jnp.int32(0)
    for a in range(n):
        index = jnp.where(me == a, table[a][1] if a in table else a, index)
    return index


def blocks_kernel(tables, n, chunks, acts, og, wt, acts_t, *rest):
    rows_v, outs = rest[:n], rest[n : 2 * n]
    acts_v, wt_v, wt_2, sems = rest[2 * n :]
    tok = acts.shape[0]
    _, cols = wt.shape
    block = tok // n
    width = cols // chunks
    me = lax.axis_index("tensor")
    places = [pl.multiple_of(pick(me, table, n) * block, block) for table in tables]

    def load(src, dst, at):
        copy = pltpu.make_async_copy(src, dst, sems.at[at])
        copy.start()
        return copy

    acts_in = [
        load(acts.at[pl.ds(at, block), :], acts_v.at[k * block : (k + 1) * block, :], k)
        for k, at in enumerate(places)
    ]
    wt_in = [
        load(wt.at[:, c * width : (c + 1) * width], wt_v.at[c], 2 * n + c) for c in range(chunks)
    ]
    rows_in = [load(og.at[pl.ds(at, block), :], rows_v[k], n + k) for k, at in enumerate(places)]
    for copy in acts_in:
        copy.wait()
    acts_t[...] = acts_v[...].T
    for c in range(chunks):
        wt_in[c].wait()
        high, low = split(wt_v[c])
        wt_2[:, c * width : (c + 1) * width] = high
        wt_2[:, cols + c * width : cols + (c + 1) * width] = low
    for copy in rows_in:
        copy.wait()
    for k in range(n):
        rows = rows_v[k][...]
        outs[k][...] = dot(jnp.concatenate([rows, rows], axis=1), wt_2[...], NT)


def blocks_of(acts, og, wt, rounds):
    n = len(rounds) + 1
    tok = og.shape[0]
    din, cols = wt.shape
    chunks = 2
    block = tok // n
    shape = jax.ShapeDtypeStruct
    out = pl.pallas_call(
        functools.partial(blocks_kernel, [{}, *rounds], n, chunks),
        out_shape=[shape((din, tok), BF16)]
        + [shape((block, cols), BF16)] * n
        + [shape((block, din), F32)] * n,
        in_specs=[HBM] * 3,
        out_specs=[VMEM] * (1 + 2 * n),
        scratch_shapes=[
            pltpu.VMEM((tok, din), BF16),
            pltpu.VMEM((chunks, din, cols // chunks), F32),
            pltpu.VMEM((din, 2 * cols), BF16),
            pltpu.SemaphoreType.DMA((2 * n + chunks,)),
        ],
        compiler_params=pltpu.CompilerParams(vmem_limit_bytes=VMEM_BYTES - SPARE),
        cost_estimate=pl.CostEstimate(
            flops=4 * tok * din * cols, bytes_accessed=4 << 20, transcendentals=0
        ),
        name="blocks",
    )(acts, og, wt)
    return out[0], out[1 : 1 + n], out[1 + n :]


def merged_kernel(acts_t, err, *rest):
    rows, (theirs, mine) = rest[:-2], rest[-2:]
    tok = acts_t.shape[1]
    half = theirs.shape[1]
    side = lax.rem(lax.axis_index("dp"), 2)
    scale = 1.0 / math.sqrt(tok)
    for where, out in ((1 - side, theirs), (side, mine)):
        span = pl.ds(pl.multiple_of(where * half, half), half)
        columns = jnp.concatenate([one[:, span] for one in rows], axis=0)
        out[...] = dot(acts_t[...], columns, NN) * scale + err[0, :, span]


def merged_of(acts_t, err, rows):
    din, cols = err.shape[1:]
    tok = acts_t.shape[1]
    return pl.pallas_call(
        merged_kernel,
        out_shape=[jax.ShapeDtypeStruct((din, cols // 2), F32)] * 2,
        in_specs=[VMEM] * (2 + len(rows)),
        out_specs=[VMEM] * 2,
        compiler_params=pltpu.CompilerParams(vmem_limit_bytes=8 << 20),
        cost_estimate=pl.CostEstimate(
            flops=2 * tok * din * cols, bytes_accessed=4 << 20, transcendentals=0
        ),
        name="merged",
    )(acts_t, err, *rows)


def is_between(n_tensor):
    me = lax.axis_index("tensor")
    return ((me == 1) | (me == n_tensor - 2)).astype(F32)


def onward_kernel(n_tensor, block, relayed, out):
    out[...] = block[...] + is_between(n_tensor) * relayed[...]


def gather_kernel(relays, first, *rest):
    total = first[...]
    if relays:
        total = total * (1.0 - is_between(relays))
    for part in rest[:-1]:
        total = total + part[...]
    rest[-1][...] = total


def summed(kernel, *parts):
    return pl.pallas_call(
        kernel,
        out_shape=jax.ShapeDtypeStruct(parts[0].shape, F32),
        in_specs=[VMEM] * len(parts),
        out_specs=VMEM,
        compiler_params=pltpu.CompilerParams(vmem_limit_bytes=4 << 20),
    )(*parts)


def left_kernel(qt, theirs, mine, o_ref):
    half = theirs.shape[1]
    side = lax.rem(lax.axis_index("dp"), 2)
    far = qt[:, pl.ds(pl.multiple_of((1 - side) * half, half), half)]
    near = qt[:, pl.ds(pl.multiple_of(side * half, half), half)]
    o_ref[...] = dot3(far, theirs[...], NT) + dot3(near, mine[...], NT)


def left_of(qt, theirs, mine):
    return pl.pallas_call(
        left_kernel,
        out_shape=jax.ShapeDtypeStruct((qt.shape[0], mine.shape[0]), F32),
        in_specs=[VMEM] * 3,
        out_specs=VMEM,
        compiler_params=pltpu.CompilerParams(vmem_limit_bytes=8 << 20),
        name="left",
    )(qt, theirs, mine)


def solve_kernel(replicas, a_ref, b_ref, y_ref):
    left = (a_ref[...] + b_ref[...]) * (1.0 / replicas)
    rank, din = left.shape
    gram = lax.dot_general(
        left, left, NT, precision=lax.Precision.HIGHEST, preferred_element_type=F32
    )
    tiles, lanes = rank // 8, 128
    spans = range(0, din, lanes)
    state = [
        [gram[8 * i : 8 * i + 8, :]] + [left[8 * i : 8 * i + 8, at : at + lanes] for at in spans]
        for i in range(tiles)
    ]
    sub = lax.broadcasted_iota(jnp.int32, (8, lanes), 0)
    for k in range(0, rank, 2):
        i, s = divmod(k, 8)
        first = [jnp.broadcast_to(row[0][:, k : k + 1], (8, lanes)) for row in state]
        second = [jnp.broadcast_to(row[0][:, k + 1 : k + 2], (8, lanes)) for row in state]
        a = first[i][s : s + 1, :]
        b = second[i][s : s + 1, :]
        d = second[i][s + 1 : s + 2, :]
        inverse = 1.0 / (a * d - b * b)
        p, q, r = d * inverse, b * inverse, a * inverse
        for part in range(len(state[0])):
            wide = state[0][part].shape[1]
            top = state[i][part][s : s + 1, :]
            low = state[i][part][s + 1 : s + 2, :]
            new_top = p[:, :wide] * top - q[:, :wide] * low
            new_low = r[:, :wide] * low - q[:, :wide] * top
            for j in range(tiles):
                old = state[j][part]
                new = old - first[j][:, :wide] * new_top - second[j][:, :wide] * new_low
                if j == i:
                    new = jnp.where(sub[:, :wide] == s, new_top, new)
                    new = jnp.where(sub[:, :wide] == s + 1, new_low, new)
                state[j][part] = new
    for j in range(tiles):
        for n, at in enumerate(spans):
            y_ref[8 * j : 8 * j + 8, at : at + lanes] = state[j][1 + n]


def solve(a, b, replicas):
    return pl.pallas_call(
        functools.partial(solve_kernel, replicas),
        out_shape=jax.ShapeDtypeStruct(a.shape, F32),
        in_specs=[VMEM] * 2,
        out_specs=VMEM,
        compiler_params=pltpu.CompilerParams(vmem_limit_bytes=4 << 20),
        cost_estimate=pl.CostEstimate(
            flops=1 << 30, bytes_accessed=1 << 20, transcendentals=0
        ),
        name="solve",
    )(a, b)


def begin_kernel(mine, came, *out):
    width = out[0].shape[1]
    for n, ref in enumerate(out):
        here = slice(n * width, (n + 1) * width)
        ref[...] = mine[:, here] + came[:, here]


def begin(mine, came):
    din, half = mine.shape
    return pl.pallas_call(
        begin_kernel,
        out_shape=[jax.ShapeDtypeStruct((din, half // 2), F32)] * 2,
        in_specs=[VMEM] * 2,
        out_specs=[VMEM] * 2,
        compiler_params=pltpu.CompilerParams(vmem_limit_bytes=4 << 20),
        name="begin",
    )(mine, came)


def right_kernel(replicas, left_a, left_b, *rest):
    out = rest[-1]
    left = (left_a[...] + left_b[...]) * (1.0 / replicas)
    width = rest[0].shape[1]
    for n in range(2):
        total = (rest[2 * n][...] + rest[2 * n + 1][...]) * (1.0 / replicas)
        out[:, n * width : (n + 1) * width] = dot3(left, total, NN)


def right_of(left, left_came, parts, replicas):
    width = parts[0].shape[1]
    return pl.pallas_call(
        functools.partial(right_kernel, replicas),
        out_shape=jax.ShapeDtypeStruct((left.shape[0], 2 * width), F32),
        in_specs=[VMEM] * 6,
        out_specs=VMEM,
        compiler_params=pltpu.CompilerParams(vmem_limit_bytes=8 << 20),
        name="right",
    )(left, left_came, *parts)


def back_kernel(near, chunks, o_ref, right, merged, wt, *rest):
    new_w, new_e, wv, ev, sems = rest[-5:]
    width = merged.shape[1] // chunks
    side = lax.rem(lax.axis_index("dp"), 2)
    base = (side if near else 1 - side) * chunks
    flipped = o_ref[...].T
    copies = []
    for c in range(chunks):
        span = pl.ds(pl.multiple_of((base + c) * width, width), width)
        here = slice(c * width, (c + 1) * width)
        delta = dot3(flipped, right[:, here], NN)
        ev[c] = merged[:, here] - delta
        wv[c] = wt[:, span] - delta
        for one in (
            pltpu.make_async_copy(ev.at[c], new_e.at[0, :, span], sems.at[2 * c]),
            pltpu.make_async_copy(wv.at[c], new_w.at[:, span], sems.at[2 * c + 1]),
        ):
            one.start()
            copies.append(one)
    for one in copies:
        one.wait()


def back(near, ortho, right, merged, wt, *kept):
    din, cols = wt.shape
    chunks = 2
    width = cols // 2 // chunks
    return pl.pallas_call(
        functools.partial(back_kernel, near, chunks),
        out_shape=[
            jax.ShapeDtypeStruct((din, cols), F32),
            jax.ShapeDtypeStruct((1, din, cols), F32),
        ],
        in_specs=[VMEM] * 4 + [ANY] * len(kept),
        out_specs=[ANY] * 2,
        input_output_aliases={4 + n: n for n in range(len(kept))},
        scratch_shapes=[
            pltpu.VMEM((chunks, din, width), F32),
            pltpu.VMEM((chunks, din, width), F32),
            pltpu.SemaphoreType.DMA((2 * chunks,)),
        ],
        compiler_params=pltpu.CompilerParams(vmem_limit_bytes=16 << 20),
        name="back_near" if near else "back_far",
    )(ortho, right, merged, wt, *kept)


def send(x, axis, pairs):
    return lax.ppermute(x, axis, pairs)


def step(acts, out_grad, weight, error, start_q):
    replicas = lax.axis_size("dp")
    n_tensor = lax.axis_size("tensor")
    bits = [1 << b for b in range(1, replicas.bit_length() - 1)]
    pair = swap(1, 1, replicas)

    table, relays = rounds_of(n_tensor)
    acts_t, rows, blocks = blocks_of(acts, out_grad, weight, table)

    def across(block, n):
        return send(block, "tensor", [(a, to) for a, (to, _) in sorted(table[n].items())])

    received = [across(blocks[1], 0)]
    theirs, mine = merged_of(acts_t, error, rows)
    came = send(theirs, "dp", pair)
    left = left_of(start_q.T, theirs, mine)
    left_came = send(left, "dp", pair)
    totals = begin(mine, came)
    comes = [None, None]
    for n, (one, other) in enumerate(zip(bits, bits[::-1]), 1):
        if n > 1:
            totals = [total + came for total, came in zip(totals, comes)]
        left = left + left_came
        left_came = send(left, "dp", swap(other, other, replicas))
        comes = [
            send(total, "dp", swap(bit, bit, replicas))
            for total, bit in zip(totals, (one, other))
        ]

    for n in range(1, n_tensor - 1):
        block = blocks[n + 1]
        if relays and n == 1:
            onward = functools.partial(onward_kernel, n_tensor)
            block = summed(onward, block, received[0])
        received.append(across(block, n))
    gather = functools.partial(gather_kernel, n_tensor if relays else None)
    input_grad = summed(gather, *received, blocks[0])

    basis = solve(left, left_came, replicas)
    parts = [totals[0], comes[0], totals[1], comes[1]]
    right = right_of(left, left_came, parts, replicas)
    other = send(right, "dp", pair)
    kept = back(True, basis, right, mine, weight)
    new_weight, new_error = back(False, basis, other, theirs, weight, *kept)
    return (new_weight, new_error, input_grad)


def solution(mesh):
    placed = (
        P("dp", None),
        P("dp", "tensor"),
        P(None, "tensor"),
        P("dp", None, "tensor"),
        P("tensor", None),
    )
    return jax.shard_map(
        step,
        mesh=mesh,
        in_specs=placed,
        out_specs=(P(None, "tensor"), P("dp", None, "tensor"), P(("dp", "tensor"), None)),
        check_vma=False,
    )
```

```python
import functools
import math

import jax
import jax.numpy as jnp
from jax import lax
from jax.experimental import pallas as pl
from jax.experimental.pallas import tpu as pltpu
from jax.sharding import PartitionSpec as P


F32 = jnp.float32
BF16 = jnp.bfloat16
NN = (((1,), (0,)), ((), ()))
NT = (((1,), (1,)), ((), ()))
VMEM_BYTES = 67043328
SPARE = 27 << 19
VMEM = pl.BlockSpec(memory_space=pltpu.VMEM)
ANY = pl.BlockSpec(memory_space=pl.ANY)
HBM = pl.BlockSpec(memory_space=pltpu.HBM)


def swap(bit_even, bit_odd, size):
    return [(i, i ^ (bit_odd if i & 1 else bit_even)) for i in range(size)]


def split(x):
    high = x.astype(BF16)
    return high, (x - high.astype(F32)).astype(BF16)


def dot(a, b, dims):
    return lax.dot_general(a, b, dims, preferred_element_type=F32)


def dot3(a, b, dims):
    (ah, al), (bh, bl) = split(a), split(b)
    return dot(ah, bh, dims) + (dot(ah, bl, dims) + dot(al, bh, dims))


def rounds_of(n):
    flows = sorted(
        ((a, b) for a in range(n) for b in range(n) if a != b),
        key=lambda flow: (abs(flow[0] - flow[1]), flow),
    )

    def fill(chosen, order):
        for a, b in list(flows)[::order]:
            if a not in chosen and all(b != to for to, _ in chosen.values()):
                chosen[a] = (b, b)
                flows.remove((a, b))
        return chosen

    relay, last = {}, {}
    if n >= 4:
        for gone in ((0, n - 2), (n - 1, 1), (1, n - 2), (n - 2, 1)):
            flows.remove(gone)
        relay = fill({0: (1, n - 2), n - 1: (n - 2, 1)}, -1)
        last = fill({1: (n - 2, n - 2), n - 2: (1, 1)}, -1)
    plain = []
    while flows:
        plain.append(fill({}, 1))
    rounds = [relay, last, *plain] if relay else plain
    if len(rounds) == n - 1 and all(len(one) == n for one in rounds):
        return rounds, bool(relay)
    return [{a: ((a + k) % n,) * 2 for a in range(n)} for k in range(1, n)], False


def pick(me, table, n):
    index = jnp.int32(0)
    for a in range(n):
        index = jnp.where(me == a, table[a][1] if a in table else a, index)
    return index


def blocks_kernel(tables, n, chunks, acts, og, wt, acts_t, *rest):
    rows_v, outs = rest[:n], rest[n : 2 * n]
    acts_v, wt_v, wt_2, sems = rest[2 * n :]
    tok = acts.shape[0]
    _, cols = wt.shape
    block = tok // n
    width = cols // chunks
    me = lax.axis_index("tensor")
    places = [pl.multiple_of(pick(me, table, n) * block, block) for table in tables]

    def load(src, dst, at):
        copy = pltpu.make_async_copy(src, dst, sems.at[at])
        copy.start()
        return copy

    acts_in = [
        load(acts.at[pl.ds(at, block), :], acts_v.at[k * block : (k + 1) * block, :], k)
        for k, at in enumerate(places)
    ]
    wt_in = [
        load(wt.at[:, c * width : (c + 1) * width], wt_v.at[c], 2 * n + c) for c in range(chunks)
    ]
    rows_in = [load(og.at[pl.ds(at, block), :], rows_v[k], n + k) for k, at in enumerate(places)]
    for copy in acts_in:
        copy.wait()
    acts_t[...] = acts_v[...].T
    for c in range(chunks):
        wt_in[c].wait()
        high, low = split(wt_v[c])
        wt_2[:, c * width : (c + 1) * width] = high
        wt_2[:, cols + c * width : cols + (c + 1) * width] = low
    for copy in rows_in:
        copy.wait()
    for k in range(n):
        rows = rows_v[k][...]
        outs[k][...] = dot(jnp.concatenate([rows, rows], axis=1), wt_2[...], NT)


def blocks_of(acts, og, wt, rounds):
    n = len(rounds) + 1
    tok = og.shape[0]
    din, cols = wt.shape
    chunks = 2
    block = tok // n
    shape = jax.ShapeDtypeStruct
    out = pl.pallas_call(
        functools.partial(blocks_kernel, [{}, *rounds], n, chunks),
        out_shape=[shape((din, tok), BF16)]
        + [shape((block, cols), BF16)] * n
        + [shape((block, din), F32)] * n,
        in_specs=[HBM] * 3,
        out_specs=[VMEM] * (1 + 2 * n),
        scratch_shapes=[
            pltpu.VMEM((tok, din), BF16),
            pltpu.VMEM((chunks, din, cols // chunks), F32),
            pltpu.VMEM((din, 2 * cols), BF16),
            pltpu.SemaphoreType.DMA((2 * n + chunks,)),
        ],
        compiler_params=pltpu.CompilerParams(vmem_limit_bytes=VMEM_BYTES - SPARE),
        cost_estimate=pl.CostEstimate(
            flops=4 * tok * din * cols, bytes_accessed=4 << 20, transcendentals=0
        ),
        name="blocks",
    )(acts, og, wt)
    return out[0], out[1 : 1 + n], out[1 + n :]


def merged_kernel(acts_t, err, *rest):
    rows, (theirs, mine) = rest[:-2], rest[-2:]
    tok = acts_t.shape[1]
    half = theirs.shape[1]
    side = lax.rem(lax.axis_index("dp"), 2)
    scale = 1.0 / math.sqrt(tok)
    for where, out in ((1 - side, theirs), (side, mine)):
        span = pl.ds(pl.multiple_of(where * half, half), half)
        columns = jnp.concatenate([one[:, span] for one in rows], axis=0)
        out[...] = dot(acts_t[...], columns, NN) * scale + err[0, :, span]


def merged_of(acts_t, err, rows):
    din, cols = err.shape[1:]
    tok = acts_t.shape[1]
    return pl.pallas_call(
        merged_kernel,
        out_shape=[jax.ShapeDtypeStruct((din, cols // 2), F32)] * 2,
        in_specs=[VMEM] * (2 + len(rows)),
        out_specs=[VMEM] * 2,
        compiler_params=pltpu.CompilerParams(vmem_limit_bytes=8 << 20),
        cost_estimate=pl.CostEstimate(
            flops=2 * tok * din * cols, bytes_accessed=4 << 20, transcendentals=0
        ),
        name="merged",
    )(acts_t, err, *rows)


def is_between(n_tensor):
    me = lax.axis_index("tensor")
    return ((me == 1) | (me == n_tensor - 2)).astype(F32)


def onward_kernel(n_tensor, block, relayed, out):
    out[...] = block[...] + is_between(n_tensor) * relayed[...]


def gather_kernel(relays, first, *rest):
    total = first[...]
    if relays:
        total = total * (1.0 - is_between(relays))
    for part in rest[:-1]:
        total = total + part[...]
    rest[-1][...] = total


def summed(kernel, *parts):
    return pl.pallas_call(
        kernel,
        out_shape=jax.ShapeDtypeStruct(parts[0].shape, F32),
        in_specs=[VMEM] * len(parts),
        out_specs=VMEM,
        compiler_params=pltpu.CompilerParams(vmem_limit_bytes=4 << 20),
    )(*parts)


def left_kernel(qt, theirs, mine, o_ref):
    half = theirs.shape[1]
    side = lax.rem(lax.axis_index("dp"), 2)
    far = qt[:, pl.ds(pl.multiple_of((1 - side) * half, half), half)]
    near = qt[:, pl.ds(pl.multiple_of(side * half, half), half)]
    o_ref[...] = dot3(far, theirs[...], NT) + dot3(near, mine[...], NT)


def left_of(qt, theirs, mine):
    return pl.pallas_call(
        left_kernel,
        out_shape=jax.ShapeDtypeStruct((qt.shape[0], mine.shape[0]), F32),
        in_specs=[VMEM] * 3,
        out_specs=VMEM,
        compiler_params=pltpu.CompilerParams(vmem_limit_bytes=8 << 20),
        name="left",
    )(qt, theirs, mine)


def solve_kernel(replicas, a_ref, b_ref, y_ref):
    left = (a_ref[...] + b_ref[...]) * (1.0 / replicas)
    rank, din = left.shape
    gram = lax.dot_general(
        left, left, NT, precision=lax.Precision.HIGHEST, preferred_element_type=F32
    )
    tiles, lanes = rank // 8, 128
    spans = range(0, din, lanes)
    state = [
        [gram[8 * i : 8 * i + 8, :]] + [left[8 * i : 8 * i + 8, at : at + lanes] for at in spans]
        for i in range(tiles)
    ]
    sub = lax.broadcasted_iota(jnp.int32, (8, lanes), 0)
    for k in range(0, rank, 2):
        i, s = divmod(k, 8)
        first = [jnp.broadcast_to(row[0][:, k : k + 1], (8, lanes)) for row in state]
        second = [jnp.broadcast_to(row[0][:, k + 1 : k + 2], (8, lanes)) for row in state]
        a = first[i][s : s + 1, :]
        b = second[i][s : s + 1, :]
        d = second[i][s + 1 : s + 2, :]
        inverse = 1.0 / (a * d - b * b)
        p, q, r = d * inverse, b * inverse, a * inverse
        for part in range(len(state[0])):
            wide = state[0][part].shape[1]
            top = state[i][part][s : s + 1, :]
            low = state[i][part][s + 1 : s + 2, :]
            new_top = p[:, :wide] * top - q[:, :wide] * low
            new_low = r[:, :wide] * low - q[:, :wide] * top
            for j in range(tiles):
                old = state[j][part]
                new = old - first[j][:, :wide] * new_top - second[j][:, :wide] * new_low
                if j == i:
                    new = jnp.where(sub[:, :wide] == s, new_top, new)
                    new = jnp.where(sub[:, :wide] == s + 1, new_low, new)
                state[j][part] = new
    for j in range(tiles):
        for n, at in enumerate(spans):
            y_ref[8 * j : 8 * j + 8, at : at + lanes] = state[j][1 + n]


def solve(a, b, replicas):
    return pl.pallas_call(
        functools.partial(solve_kernel, replicas),
        out_shape=jax.ShapeDtypeStruct(a.shape, F32),
        in_specs=[VMEM] * 2,
        out_specs=VMEM,
        compiler_params=pltpu.CompilerParams(vmem_limit_bytes=4 << 20),
        cost_estimate=pl.CostEstimate(
            flops=1 << 30, bytes_accessed=1 << 20, transcendentals=0
        ),
        name="solve",
    )(a, b)


def quarter(bits, side, index):
    even, odd = (lax.rem(index // bit, 2) for bit in (bits[0], bits[-1]))
    return jnp.where(side == 0, even, odd)


def begin_kernel(bits, mine, came, keep, give):
    width = keep.shape[1]
    index = lax.axis_index("dp")
    own = quarter(bits, lax.rem(index, 2), index)
    for which, out in ((own, keep), (1 - own, give)):
        span = pl.ds(pl.multiple_of(which * width, width), width)
        out[...] = mine[:, span] + came[:, span]


def begin(mine, came, bits):
    din, half = mine.shape
    return pl.pallas_call(
        functools.partial(begin_kernel, bits),
        out_shape=[jax.ShapeDtypeStruct((din, half // 2), F32)] * 2,
        in_specs=[VMEM] * 2,
        out_specs=[VMEM] * 2,
        compiler_params=pltpu.CompilerParams(vmem_limit_bytes=4 << 20),
        name="begin",
    )(mine, came)


def right_kernel(replicas, left_a, left_b, total_a, total_b, out):
    left = (left_a[...] + left_b[...]) * (1.0 / replicas)
    out[...] = dot3(left, (total_a[...] + total_b[...]) * (1.0 / replicas), NN)


def right_of(left, left_came, total, came, replicas):
    return pl.pallas_call(
        functools.partial(right_kernel, replicas),
        out_shape=jax.ShapeDtypeStruct((left.shape[0], total.shape[1]), F32),
        in_specs=[VMEM] * 4,
        out_specs=VMEM,
        compiler_params=pltpu.CompilerParams(vmem_limit_bytes=8 << 20),
        name="right",
    )(left, left_came, total, came)


def back_kernel(near, bits, basis, right_a, right_b, merged, wt, *rest):
    new_w, new_e, wv, ev, sems = rest[-5:]
    width = right_a.shape[1]
    index = lax.axis_index("dp")
    side = lax.rem(index, 2)
    side = side if near else 1 - side
    own = quarter(bits, side, index)
    flipped = basis[...].T
    copies = []
    for c, (right, which) in enumerate(((right_a, own), (right_b, 1 - own))):
        here = pl.ds(pl.multiple_of(which * width, width), width)
        span = pl.ds(pl.multiple_of((2 * side + which) * width, width), width)
        delta = dot3(flipped, right[...], NN)
        ev[c] = merged[:, here] - delta
        wv[c] = wt[:, span] - delta
        for one in (
            pltpu.make_async_copy(ev.at[c], new_e.at[0, :, span], sems.at[2 * c]),
            pltpu.make_async_copy(wv.at[c], new_w.at[:, span], sems.at[2 * c + 1]),
        ):
            one.start()
            copies.append(one)
    for one in copies:
        one.wait()


def back(near, bits, basis, right_a, right_b, merged, wt, *kept):
    din, cols = wt.shape
    width = right_a.shape[1]
    return pl.pallas_call(
        functools.partial(back_kernel, near, bits),
        out_shape=[
            jax.ShapeDtypeStruct((din, cols), F32),
            jax.ShapeDtypeStruct((1, din, cols), F32),
        ],
        in_specs=[VMEM] * 5 + [ANY] * len(kept),
        out_specs=[ANY] * 2,
        input_output_aliases={5 + n: n for n in range(len(kept))},
        scratch_shapes=[
            pltpu.VMEM((2, din, width), F32),
            pltpu.VMEM((2, din, width), F32),
            pltpu.SemaphoreType.DMA((4,)),
        ],
        compiler_params=pltpu.CompilerParams(vmem_limit_bytes=16 << 20),
        name="back_near" if near else "back_far",
    )(basis, right_a, right_b, merged, wt, *kept)


def send(x, axis, pairs):
    return lax.ppermute(x, axis, pairs)


def step(acts, out_grad, weight, error, start_q):
    replicas = lax.axis_size("dp")
    n_tensor = lax.axis_size("tensor")
    bits = [1 << b for b in range(1, replicas.bit_length() - 1)]
    pair = swap(1, 1, replicas)

    table, relays = rounds_of(n_tensor)
    acts_t, rows, blocks = blocks_of(acts, out_grad, weight, table)

    def across(block, n):
        return send(block, "tensor", [(a, to) for a, (to, _) in sorted(table[n].items())])

    received = [across(blocks[1], 0)]
    theirs, mine = merged_of(acts_t, error, rows)
    came = send(theirs, "dp", pair)
    left = left_of(start_q.T, theirs, mine)
    total, give = begin(mine, came, bits)
    came = send(give, "dp", swap(bits[0], bits[-1], replicas))
    left = left + send(left, "dp", swap(bits[-1], bits[0], replicas))
    for n, (one, other) in enumerate(zip(bits[1:], bits[-2::-1]), 2):
        total = total + came
        came = send(total, "dp", swap(one, other, replicas))
        left = left + send(left, "dp", swap(other, one, replicas))
    left_came = send(left, "dp", pair)

    for n in range(1, n_tensor - 1):
        block = blocks[n + 1]
        if relays and n == 1:
            onward = functools.partial(onward_kernel, n_tensor)
            block = summed(onward, block, received[0])
        received.append(across(block, n))
    gather = functools.partial(gather_kernel, n_tensor if relays else None)
    input_grad = summed(gather, *received, blocks[0])

    right = right_of(left, left_came, total, came, replicas)
    beside = send(right, "dp", swap(bits[0], bits[-1], replicas))
    across_pair = send(right, "dp", pair)
    basis = solve(left, left_came, replicas)
    beside_across = send(beside, "dp", pair)
    kept = back(True, bits, basis, right, beside, mine, weight)
    new_weight, new_error = back(
        False, bits, basis, across_pair, beside_across, theirs, weight, *kept
    )
    return (new_weight, new_error, input_grad)


def solution(mesh):
    placed = (
        P("dp", None),
        P("dp", "tensor"),
        P(None, "tensor"),
        P("dp", None, "tensor"),
        P("tensor", None),
    )
    return jax.shard_map(
        step,
        mesh=mesh,
        in_specs=placed,
        out_specs=(P(None, "tensor"), P("dp", None, "tensor"), P(("dp", "tensor"), None)),
        check_vma=False,
    )
```

```python
import functools
import math

import jax
import jax.numpy as jnp
from jax import lax
from jax.experimental import pallas as pl
from jax.experimental.pallas import tpu as pltpu
from jax.sharding import PartitionSpec as P


F32 = jnp.float32
BF16 = jnp.bfloat16
NN = (((1,), (0,)), ((), ()))
NT = (((1,), (1,)), ((), ()))
VMEM_BYTES = 67043328
SPARE = 27 << 19
VMEM = pl.BlockSpec(memory_space=pltpu.VMEM)
ANY = pl.BlockSpec(memory_space=pl.ANY)
HBM = pl.BlockSpec(memory_space=pltpu.HBM)


def swap(bit_even, bit_odd, size):
    return [(i, i ^ (bit_odd if i & 1 else bit_even)) for i in range(size)]


def split(x):
    high = x.astype(BF16)
    return high, (x - high.astype(F32)).astype(BF16)


def dot(a, b, dims):
    return lax.dot_general(a, b, dims, preferred_element_type=F32)


def dot3(a, b, dims):
    (ah, al), (bh, bl) = split(a), split(b)
    return dot(ah, bh, dims) + (dot(ah, bl, dims) + dot(al, bh, dims))


def rounds_of(n):
    flows = sorted(
        ((a, b) for a in range(n) for b in range(n) if a != b),
        key=lambda flow: (abs(flow[0] - flow[1]), flow),
    )

    def fill(chosen, order):
        for a, b in list(flows)[::order]:
            if a not in chosen and all(b != to for to, _ in chosen.values()):
                chosen[a] = (b, b)
                flows.remove((a, b))
        return chosen

    relay, last = {}, {}
    if n >= 4:
        for gone in ((0, n - 2), (n - 1, 1), (1, n - 2), (n - 2, 1)):
            flows.remove(gone)
        relay = fill({0: (1, n - 2), n - 1: (n - 2, 1)}, -1)
        last = fill({1: (n - 2, n - 2), n - 2: (1, 1)}, -1)
    plain = []
    while flows:
        plain.append(fill({}, 1))
    rounds = [relay, last, *plain] if relay else plain
    if len(rounds) == n - 1 and all(len(one) == n for one in rounds):
        return rounds, bool(relay)
    return [{a: ((a + k) % n,) * 2 for a in range(n)} for k in range(1, n)], False


def pick(me, table, n):
    index = jnp.int32(0)
    for a in range(n):
        index = jnp.where(me == a, table[a][1] if a in table else a, index)
    return index


def blocks_kernel(tables, n, chunks, acts, og, wt, acts_t, *rest):
    rows_v, outs = rest[:n], rest[n : 2 * n]
    acts_v, wt_v, wt_2, sems = rest[2 * n :]
    tok = acts.shape[0]
    _, cols = wt.shape
    block = tok // n
    width = cols // chunks
    me = lax.axis_index("tensor")
    places = [pl.multiple_of(pick(me, table, n) * block, block) for table in tables]

    def load(src, dst, at):
        copy = pltpu.make_async_copy(src, dst, sems.at[at])
        copy.start()
        return copy

    acts_in = [
        load(acts.at[pl.ds(at, block), :], acts_v.at[k * block : (k + 1) * block, :], k)
        for k, at in enumerate(places)
    ]
    wt_in = [
        load(wt.at[:, c * width : (c + 1) * width], wt_v.at[c], 2 * n + c) for c in range(chunks)
    ]
    rows_in = [load(og.at[pl.ds(at, block), :], rows_v[k], n + k) for k, at in enumerate(places)]
    for copy in acts_in:
        copy.wait()
    acts_t[...] = acts_v[...].T
    for c in range(chunks):
        wt_in[c].wait()
        high, low = split(wt_v[c])
        wt_2[:, c * width : (c + 1) * width] = high
        wt_2[:, cols + c * width : cols + (c + 1) * width] = low
    for copy in rows_in:
        copy.wait()
    for k in range(n):
        rows = rows_v[k][...]
        outs[k][...] = dot(jnp.concatenate([rows, rows], axis=1), wt_2[...], NT)


def blocks_of(acts, og, wt, rounds):
    n = len(rounds) + 1
    tok = og.shape[0]
    din, cols = wt.shape
    chunks = 2
    block = tok // n
    shape = jax.ShapeDtypeStruct
    out = pl.pallas_call(
        functools.partial(blocks_kernel, [{}, *rounds], n, chunks),
        out_shape=[shape((din, tok), BF16)]
        + [shape((block, cols), BF16)] * n
        + [shape((block, din), F32)] * n,
        in_specs=[HBM] * 3,
        out_specs=[VMEM] * (1 + 2 * n),
        scratch_shapes=[
            pltpu.VMEM((tok, din), BF16),
            pltpu.VMEM((chunks, din, cols // chunks), F32),
            pltpu.VMEM((din, 2 * cols), BF16),
            pltpu.SemaphoreType.DMA((2 * n + chunks,)),
        ],
        compiler_params=pltpu.CompilerParams(vmem_limit_bytes=VMEM_BYTES - SPARE),
        cost_estimate=pl.CostEstimate(
            flops=4 * tok * din * cols, bytes_accessed=4 << 20, transcendentals=0
        ),
        name="blocks",
    )(acts, og, wt)
    return out[0], out[1 : 1 + n], out[1 + n :]


def merged_kernel(acts_t, err, *rest):
    rows, (theirs, mine) = rest[:-2], rest[-2:]
    tok = acts_t.shape[1]
    half = theirs.shape[1]
    side = lax.rem(lax.axis_index("dp"), 2)
    scale = 1.0 / math.sqrt(tok)
    for where, out in ((1 - side, theirs), (side, mine)):
        span = pl.ds(pl.multiple_of(where * half, half), half)
        columns = jnp.concatenate([one[:, span] for one in rows], axis=0)
        out[...] = dot(acts_t[...], columns, NN) * scale + err[0, :, span]


def merged_of(acts_t, err, rows):
    din, cols = err.shape[1:]
    tok = acts_t.shape[1]
    return pl.pallas_call(
        merged_kernel,
        out_shape=[jax.ShapeDtypeStruct((din, cols // 2), F32)] * 2,
        in_specs=[VMEM] * (2 + len(rows)),
        out_specs=[VMEM] * 2,
        compiler_params=pltpu.CompilerParams(vmem_limit_bytes=8 << 20),
        cost_estimate=pl.CostEstimate(
            flops=2 * tok * din * cols, bytes_accessed=4 << 20, transcendentals=0
        ),
        name="merged",
    )(acts_t, err, *rows)


def is_between(n_tensor):
    me = lax.axis_index("tensor")
    return ((me == 1) | (me == n_tensor - 2)).astype(F32)


def onward_kernel(n_tensor, block, relayed, out):
    out[...] = block[...] + is_between(n_tensor) * relayed[...]


def gather_kernel(relays, first, *rest):
    total = first[...]
    if relays:
        total = total * (1.0 - is_between(relays))
    for part in rest[:-1]:
        total = total + part[...]
    rest[-1][...] = total


def summed(kernel, *parts):
    return pl.pallas_call(
        kernel,
        out_shape=jax.ShapeDtypeStruct(parts[0].shape, F32),
        in_specs=[VMEM] * len(parts),
        out_specs=VMEM,
        compiler_params=pltpu.CompilerParams(vmem_limit_bytes=4 << 20),
    )(*parts)


def left_kernel(qt, theirs, mine, o_ref):
    half = theirs.shape[1]
    side = lax.rem(lax.axis_index("dp"), 2)
    far = qt[:, pl.ds(pl.multiple_of((1 - side) * half, half), half)]
    near = qt[:, pl.ds(pl.multiple_of(side * half, half), half)]
    o_ref[...] = dot3(far, theirs[...], NT) + dot3(near, mine[...], NT)


def left_of(qt, theirs, mine):
    return pl.pallas_call(
        left_kernel,
        out_shape=jax.ShapeDtypeStruct((qt.shape[0], mine.shape[0]), F32),
        in_specs=[VMEM] * 3,
        out_specs=VMEM,
        compiler_params=pltpu.CompilerParams(vmem_limit_bytes=8 << 20),
        name="left",
    )(qt, theirs, mine)


def solve_kernel(replicas, a_ref, b_ref, y_ref):
    left = (a_ref[...] + b_ref[...]) * (1.0 / replicas)
    rank, din = left.shape
    gram = lax.dot_general(
        left, left, NT, precision=lax.Precision.HIGHEST, preferred_element_type=F32
    )
    tiles, lanes = rank // 8, 128
    spans = range(0, din, lanes)
    state = [
        [gram[8 * i : 8 * i + 8, :]] + [left[8 * i : 8 * i + 8, at : at + lanes] for at in spans]
        for i in range(tiles)
    ]
    sub = lax.broadcasted_iota(jnp.int32, (8, lanes), 0)
    for k in range(0, rank, 2):
        i, s = divmod(k, 8)
        first = [jnp.broadcast_to(row[0][:, k : k + 1], (8, lanes)) for row in state]
        second = [jnp.broadcast_to(row[0][:, k + 1 : k + 2], (8, lanes)) for row in state]
        a = first[i][s : s + 1, :]
        b = second[i][s : s + 1, :]
        d = second[i][s + 1 : s + 2, :]
        inverse = 1.0 / (a * d - b * b)
        p, q, r = d * inverse, b * inverse, a * inverse
        for part in range(len(state[0])):
            wide = state[0][part].shape[1]
            top = state[i][part][s : s + 1, :]
            low = state[i][part][s + 1 : s + 2, :]
            new_top = p[:, :wide] * top - q[:, :wide] * low
            new_low = r[:, :wide] * low - q[:, :wide] * top
            for j in range(tiles):
                old = state[j][part]
                new = old - first[j][:, :wide] * new_top - second[j][:, :wide] * new_low
                if j == i:
                    new = jnp.where(sub[:, :wide] == s, new_top, new)
                    new = jnp.where(sub[:, :wide] == s + 1, new_low, new)
                state[j][part] = new
    for j in range(tiles):
        for n, at in enumerate(spans):
            y_ref[8 * j : 8 * j + 8, at : at + lanes] = state[j][1 + n]


def solve(a, b, replicas):
    return pl.pallas_call(
        functools.partial(solve_kernel, replicas),
        out_shape=jax.ShapeDtypeStruct(a.shape, F32),
        in_specs=[VMEM] * 2,
        out_specs=VMEM,
        compiler_params=pltpu.CompilerParams(vmem_limit_bytes=4 << 20),
        cost_estimate=pl.CostEstimate(
            flops=1 << 30, bytes_accessed=1 << 20, transcendentals=0
        ),
        name="solve",
    )(a, b)


def quarter(bits, side, index):
    even, odd = (lax.rem(index // bit, 2) for bit in (bits[0], bits[-1]))
    return jnp.where(side == 0, even, odd)


def begin_kernel(bits, mine, came, keep, give):
    width = keep.shape[1]
    index = lax.axis_index("dp")
    own = quarter(bits, lax.rem(index, 2), index)
    for which, out in ((own, keep), (1 - own, give)):
        span = pl.ds(pl.multiple_of(which * width, width), width)
        out[...] = mine[:, span] + came[:, span]


def begin(mine, came, bits):
    din, half = mine.shape
    return pl.pallas_call(
        functools.partial(begin_kernel, bits),
        out_shape=[jax.ShapeDtypeStruct((din, half // 2), F32)] * 2,
        in_specs=[VMEM] * 2,
        out_specs=[VMEM] * 2,
        compiler_params=pltpu.CompilerParams(vmem_limit_bytes=4 << 20),
        name="begin",
    )(mine, came)


def right_kernel(replicas, left_a, left_b, total_a, total_b, out):
    left = (left_a[...] + left_b[...]) * (1.0 / replicas)
    out[...] = dot3(left, (total_a[...] + total_b[...]) * (1.0 / replicas), NN)


def right_of(left, left_came, total, came, replicas):
    return pl.pallas_call(
        functools.partial(right_kernel, replicas),
        out_shape=jax.ShapeDtypeStruct((left.shape[0], total.shape[1]), F32),
        in_specs=[VMEM] * 4,
        out_specs=VMEM,
        compiler_params=pltpu.CompilerParams(vmem_limit_bytes=8 << 20),
        name="right",
    )(left, left_came, total, came)


def back_kernel(pieces, bits, basis, wt, *rest):
    count = len(pieces)
    rights, merged = rest[:count], rest[count : 2 * count]
    new_w, new_e, wv, ev, sems = rest[-5:]
    width = rights[0].shape[1]
    index = lax.axis_index("dp")
    flipped = basis[...].T
    copies = []
    for c, (near, same) in enumerate(pieces):
        side = lax.rem(index, 2)
        side = side if near else 1 - side
        own = quarter(bits, side, index)
        which = own if same else 1 - own
        here = pl.ds(pl.multiple_of(which * width, width), width)
        span = pl.ds(pl.multiple_of((2 * side + which) * width, width), width)
        delta = dot3(flipped, rights[c][...], NN)
        ev[c] = merged[c][:, here] - delta
        wv[c] = wt[:, span] - delta
        for one in (
            pltpu.make_async_copy(ev.at[c], new_e.at[0, :, span], sems.at[2 * c]),
            pltpu.make_async_copy(wv.at[c], new_w.at[:, span], sems.at[2 * c + 1]),
        ):
            one.start()
            copies.append(one)
    for one in copies:
        one.wait()


def back(pieces, bits, basis, wt, rights, merged, *kept):
    din, cols = wt.shape
    count = len(pieces)
    width = rights[0].shape[1]
    first = 2 + 2 * count
    return pl.pallas_call(
        functools.partial(back_kernel, pieces, bits),
        out_shape=[
            jax.ShapeDtypeStruct((din, cols), F32),
            jax.ShapeDtypeStruct((1, din, cols), F32),
        ],
        in_specs=[VMEM] * first + [ANY] * len(kept),
        out_specs=[ANY] * 2,
        input_output_aliases={first + n: n for n in range(len(kept))},
        scratch_shapes=[
            pltpu.VMEM((count, din, width), F32),
            pltpu.VMEM((count, din, width), F32),
            pltpu.SemaphoreType.DMA((2 * count,)),
        ],
        compiler_params=pltpu.CompilerParams(vmem_limit_bytes=16 << 20),
    )(basis, wt, *rights, *merged, *kept)


def send(x, axis, pairs):
    return lax.ppermute(x, axis, pairs)


def step(acts, out_grad, weight, error, start_q):
    replicas = lax.axis_size("dp")
    n_tensor = lax.axis_size("tensor")
    bits = [1 << b for b in range(1, replicas.bit_length() - 1)]
    pair = swap(1, 1, replicas)

    table, relays = rounds_of(n_tensor)
    acts_t, rows, blocks = blocks_of(acts, out_grad, weight, table)

    def across(block, n):
        return send(block, "tensor", [(a, to) for a, (to, _) in sorted(table[n].items())])

    received = [across(blocks[1], 0)]
    theirs, mine = merged_of(acts_t, error, rows)
    came = send(theirs, "dp", pair)
    left = left_of(start_q.T, theirs, mine)
    total, give = begin(mine, came, bits)
    came = send(give, "dp", swap(bits[0], bits[-1], replicas))
    left = left + send(left, "dp", swap(bits[-1], bits[0], replicas))
    for n, (one, other) in enumerate(zip(bits[1:], bits[-2::-1]), 2):
        total = total + came
        came = send(total, "dp", swap(one, other, replicas))
        left = left + send(left, "dp", swap(other, one, replicas))
    left_came = send(left, "dp", pair)

    for n in range(1, n_tensor - 1):
        block = blocks[n + 1]
        if relays and n == 1:
            onward = functools.partial(onward_kernel, n_tensor)
            block = summed(onward, block, received[0])
        received.append(across(block, n))
    gather = functools.partial(gather_kernel, n_tensor if relays else None)
    input_grad = summed(gather, *received, blocks[0])

    basis = solve(left, left_came, replicas)
    right = right_of(left, left_came, total, came, replicas)
    beside = send(right, "dp", swap(bits[0], bits[-1], replicas))
    diagonal = send(right, "dp", swap(bits[0] | 1, bits[-1] | 1, replicas))
    across_pair = send(right, "dp", pair)
    pieces = ((True, True), (True, False), (False, True))
    rights = (right, beside, across_pair)
    kept = back(pieces, bits, basis, weight, rights, (mine, mine, theirs))
    new_weight, new_error = back(
        ((False, False),), bits, basis, weight, (diagonal,), (theirs,), *kept
    )
    return (new_weight, new_error, input_grad)


def solution(mesh):
    placed = (
        P("dp", None),
        P("dp", "tensor"),
        P(None, "tensor"),
        P("dp", None, "tensor"),
        P("tensor", None),
    )
    return jax.shard_map(
        step,
        mesh=mesh,
        in_specs=placed,
        out_specs=(P(None, "tensor"), P("dp", None, "tensor"), P(("dp", "tensor"), None)),
        check_vma=False,
    )
```

```python
import functools
import math

import jax
import jax.numpy as jnp
from jax import lax
from jax.experimental import pallas as pl
from jax.experimental.pallas import tpu as pltpu
from jax.sharding import PartitionSpec as P


F32 = jnp.float32
BF16 = jnp.bfloat16
NN = (((1,), (0,)), ((), ()))
NT = (((1,), (1,)), ((), ()))
VMEM_BYTES = 67043328
SPARE = 27 << 19
VMEM = pl.BlockSpec(memory_space=pltpu.VMEM)
ANY = pl.BlockSpec(memory_space=pl.ANY)
HBM = pl.BlockSpec(memory_space=pltpu.HBM)


def swap(bit_even, bit_odd, size):
    return [(i, i ^ (bit_odd if i & 1 else bit_even)) for i in range(size)]


def split(x):
    high = x.astype(BF16)
    return high, (x - high.astype(F32)).astype(BF16)


def dot(a, b, dims):
    return lax.dot_general(a, b, dims, preferred_element_type=F32)


def dot3(a, b, dims):
    (ah, al), (bh, bl) = split(a), split(b)
    return dot(ah, bh, dims) + (dot(ah, bl, dims) + dot(al, bh, dims))


def rounds_of(n):
    flows = sorted(
        ((a, b) for a in range(n) for b in range(n) if a != b),
        key=lambda flow: (abs(flow[0] - flow[1]), flow),
    )

    def fill(chosen, order):
        for a, b in list(flows)[::order]:
            if a not in chosen and all(b != to for to, _ in chosen.values()):
                chosen[a] = (b, b)
                flows.remove((a, b))
        return chosen

    relay, last = {}, {}
    if n >= 4:
        for gone in ((0, n - 2), (n - 1, 1), (1, n - 2), (n - 2, 1)):
            flows.remove(gone)
        relay = fill({0: (1, n - 2), n - 1: (n - 2, 1)}, -1)
        last = fill({1: (n - 2, n - 2), n - 2: (1, 1)}, -1)
    plain = []
    while flows:
        plain.append(fill({}, 1))
    rounds = [relay, last, *plain] if relay else plain
    if len(rounds) == n - 1 and all(len(one) == n for one in rounds):
        return rounds, bool(relay)
    return [{a: ((a + k) % n,) * 2 for a in range(n)} for k in range(1, n)], False


def pick(me, table, n):
    index = jnp.int32(0)
    for a in range(n):
        index = jnp.where(me == a, table[a][1] if a in table else a, index)
    return index


def blocks_kernel(tables, n, chunks, acts, og, wt, acts_t, *rest):
    rows_v, outs = rest[:n], rest[n : 2 * n]
    acts_v, wt_v, wt_2, sems = rest[2 * n :]
    tok = acts.shape[0]
    _, cols = wt.shape
    block = tok // n
    width = cols // chunks
    me = lax.axis_index("tensor")
    places = [pl.multiple_of(pick(me, table, n) * block, block) for table in tables]

    def load(src, dst, at):
        copy = pltpu.make_async_copy(src, dst, sems.at[at])
        copy.start()
        return copy

    acts_in = [
        load(acts.at[pl.ds(at, block), :], acts_v.at[k * block : (k + 1) * block, :], k)
        for k, at in enumerate(places)
    ]
    wt_in = [
        load(wt.at[:, c * width : (c + 1) * width], wt_v.at[c], 2 * n + c) for c in range(chunks)
    ]
    rows_in = [load(og.at[pl.ds(at, block), :], rows_v[k], n + k) for k, at in enumerate(places)]
    for copy in acts_in:
        copy.wait()
    acts_t[...] = acts_v[...].T
    for c in range(chunks):
        wt_in[c].wait()
        high, low = split(wt_v[c])
        wt_2[:, c * width : (c + 1) * width] = high
        wt_2[:, cols + c * width : cols + (c + 1) * width] = low
    for copy in rows_in:
        copy.wait()
    for k in range(n):
        rows = rows_v[k][...]
        outs[k][...] = dot(jnp.concatenate([rows, rows], axis=1), wt_2[...], NT)


def blocks_of(acts, og, wt, rounds):
    n = len(rounds) + 1
    tok = og.shape[0]
    din, cols = wt.shape
    chunks = 2
    block = tok // n
    shape = jax.ShapeDtypeStruct
    out = pl.pallas_call(
        functools.partial(blocks_kernel, [{}, *rounds], n, chunks),
        out_shape=[shape((din, tok), BF16)]
        + [shape((block, cols), BF16)] * n
        + [shape((block, din), F32)] * n,
        in_specs=[HBM] * 3,
        out_specs=[VMEM] * (1 + 2 * n),
        scratch_shapes=[
            pltpu.VMEM((tok, din), BF16),
            pltpu.VMEM((chunks, din, cols // chunks), F32),
            pltpu.VMEM((din, 2 * cols), BF16),
            pltpu.SemaphoreType.DMA((2 * n + chunks,)),
        ],
        compiler_params=pltpu.CompilerParams(vmem_limit_bytes=VMEM_BYTES - SPARE),
        cost_estimate=pl.CostEstimate(
            flops=4 * tok * din * cols, bytes_accessed=4 << 20, transcendentals=0
        ),
        name="blocks",
    )(acts, og, wt)
    return out[0], out[1 : 1 + n], out[1 + n :]


def merged_kernel(acts_t, err, *rest):
    rows, (theirs, mine) = rest[:-2], rest[-2:]
    tok = acts_t.shape[1]
    half = theirs.shape[1]
    side = lax.rem(lax.axis_index("dp"), 2)
    scale = 1.0 / math.sqrt(tok)
    for where, out in ((1 - side, theirs), (side, mine)):
        span = pl.ds(pl.multiple_of(where * half, half), half)
        columns = jnp.concatenate([one[:, span] for one in rows], axis=0)
        out[...] = dot(acts_t[...], columns, NN) * scale + err[0, :, span]


def merged_of(acts_t, err, rows):
    din, cols = err.shape[1:]
    tok = acts_t.shape[1]
    return pl.pallas_call(
        merged_kernel,
        out_shape=[jax.ShapeDtypeStruct((din, cols // 2), F32)] * 2,
        in_specs=[VMEM] * (2 + len(rows)),
        out_specs=[VMEM] * 2,
        compiler_params=pltpu.CompilerParams(vmem_limit_bytes=8 << 20),
        cost_estimate=pl.CostEstimate(
            flops=2 * tok * din * cols, bytes_accessed=4 << 20, transcendentals=0
        ),
        name="merged",
    )(acts_t, err, *rows)


def is_between(n_tensor):
    me = lax.axis_index("tensor")
    return ((me == 1) | (me == n_tensor - 2)).astype(F32)


def onward_kernel(n_tensor, block, relayed, out):
    out[...] = block[...] + is_between(n_tensor) * relayed[...]


def gather_kernel(relays, first, *rest):
    total = first[...]
    if relays:
        total = total * (1.0 - is_between(relays))
    for part in rest[:-1]:
        total = total + part[...]
    rest[-1][...] = total


def summed(kernel, *parts):
    return pl.pallas_call(
        kernel,
        out_shape=jax.ShapeDtypeStruct(parts[0].shape, F32),
        in_specs=[VMEM] * len(parts),
        out_specs=VMEM,
        compiler_params=pltpu.CompilerParams(vmem_limit_bytes=4 << 20),
    )(*parts)


def left_kernel(qt, theirs, mine, o_ref):
    half = theirs.shape[1]
    side = lax.rem(lax.axis_index("dp"), 2)
    far = qt[:, pl.ds(pl.multiple_of((1 - side) * half, half), half)]
    near = qt[:, pl.ds(pl.multiple_of(side * half, half), half)]
    o_ref[...] = dot3(far, theirs[...], NT) + dot3(near, mine[...], NT)


def left_of(qt, theirs, mine):
    return pl.pallas_call(
        left_kernel,
        out_shape=jax.ShapeDtypeStruct((qt.shape[0], mine.shape[0]), F32),
        in_specs=[VMEM] * 3,
        out_specs=VMEM,
        compiler_params=pltpu.CompilerParams(vmem_limit_bytes=8 << 20),
        name="left",
    )(qt, theirs, mine)


def solve_kernel(replicas, a_ref, b_ref, y_ref):
    left = (a_ref[...] + b_ref[...]) * (1.0 / replicas)
    rank, din = left.shape
    gram = lax.dot_general(
        left, left, NT, precision=lax.Precision.HIGHEST, preferred_element_type=F32
    )
    tiles, lanes = rank // 8, 128
    spans = range(0, din, lanes)
    state = [
        [gram[8 * i : 8 * i + 8, :]] + [left[8 * i : 8 * i + 8, at : at + lanes] for at in spans]
        for i in range(tiles)
    ]
    sub = lax.broadcasted_iota(jnp.int32, (8, lanes), 0)
    for k in range(0, rank, 2):
        i, s = divmod(k, 8)
        first = [jnp.broadcast_to(row[0][:, k : k + 1], (8, lanes)) for row in state]
        second = [jnp.broadcast_to(row[0][:, k + 1 : k + 2], (8, lanes)) for row in state]
        a = first[i][s : s + 1, :]
        b = second[i][s : s + 1, :]
        d = second[i][s + 1 : s + 2, :]
        inverse = 1.0 / (a * d - b * b)
        p, q, r = d * inverse, b * inverse, a * inverse
        for part in range(len(state[0])):
            wide = state[0][part].shape[1]
            top = state[i][part][s : s + 1, :]
            low = state[i][part][s + 1 : s + 2, :]
            new_top = p[:, :wide] * top - q[:, :wide] * low
            new_low = r[:, :wide] * low - q[:, :wide] * top
            for j in range(tiles):
                old = state[j][part]
                new = old - first[j][:, :wide] * new_top - second[j][:, :wide] * new_low
                if j == i:
                    new = jnp.where(sub[:, :wide] == s, new_top, new)
                    new = jnp.where(sub[:, :wide] == s + 1, new_low, new)
                state[j][part] = new
    for j in range(tiles):
        for n, at in enumerate(spans):
            y_ref[8 * j : 8 * j + 8, at : at + lanes] = state[j][1 + n]


def solve(a, b, replicas):
    return pl.pallas_call(
        functools.partial(solve_kernel, replicas),
        out_shape=jax.ShapeDtypeStruct(a.shape, F32),
        in_specs=[VMEM] * 2,
        out_specs=VMEM,
        compiler_params=pltpu.CompilerParams(vmem_limit_bytes=4 << 20),
        cost_estimate=pl.CostEstimate(
            flops=1 << 30, bytes_accessed=1 << 20, transcendentals=0
        ),
        name="solve",
    )(a, b)


def quarter(bits, side, index):
    even, odd = (lax.rem(index // bit, 2) for bit in (bits[0], bits[-1]))
    return jnp.where(side == 0, even, odd)


def begin_kernel(bits, mine, came, keep, give):
    width = keep.shape[1]
    index = lax.axis_index("dp")
    own = quarter(bits, lax.rem(index, 2), index)
    for which, out in ((own, keep), (1 - own, give)):
        span = pl.ds(pl.multiple_of(which * width, width), width)
        out[...] = mine[:, span] + came[:, span]


def begin(mine, came, bits):
    din, half = mine.shape
    return pl.pallas_call(
        functools.partial(begin_kernel, bits),
        out_shape=[jax.ShapeDtypeStruct((din, half // 2), F32)] * 2,
        in_specs=[VMEM] * 2,
        out_specs=[VMEM] * 2,
        compiler_params=pltpu.CompilerParams(vmem_limit_bytes=4 << 20),
        name="begin",
    )(mine, came)


def right_kernel(replicas, left_a, left_b, total_a, total_b, out):
    left = (left_a[...] + left_b[...]) * (1.0 / replicas)
    out[...] = dot3(left, (total_a[...] + total_b[...]) * (1.0 / replicas), NN)


def right_of(left, left_came, total, came, replicas):
    return pl.pallas_call(
        functools.partial(right_kernel, replicas),
        out_shape=jax.ShapeDtypeStruct((left.shape[0], total.shape[1]), F32),
        in_specs=[VMEM] * 4,
        out_specs=VMEM,
        compiler_params=pltpu.CompilerParams(vmem_limit_bytes=8 << 20),
        name="right",
    )(left, left_came, total, came)


def back_kernel(pieces, bits, basis, wt, *rest):
    count = len(pieces)
    rights, merged = rest[:count], rest[count : 2 * count]
    new_w, new_e, wv, ev, sems = rest[-5:]
    width = rights[0].shape[1]
    index = lax.axis_index("dp")
    flipped = basis[...].T
    copies = []
    for c, (near, same) in enumerate(pieces):
        side = lax.rem(index, 2)
        side = side if near else 1 - side
        own = quarter(bits, side, index)
        which = own if same else 1 - own
        here = pl.ds(pl.multiple_of(which * width, width), width)
        span = pl.ds(pl.multiple_of((2 * side + which) * width, width), width)
        delta = dot3(flipped, rights[c][...], NN)
        ev[c] = merged[c][:, here] - delta
        wv[c] = wt[:, span] - delta
        for one in (
            pltpu.make_async_copy(ev.at[c], new_e.at[0, :, span], sems.at[2 * c]),
            pltpu.make_async_copy(wv.at[c], new_w.at[:, span], sems.at[2 * c + 1]),
        ):
            one.start()
            copies.append(one)
    for one in copies:
        one.wait()


def back(pieces, bits, basis, wt, rights, merged, *kept):
    din, cols = wt.shape
    count = len(pieces)
    width = rights[0].shape[1]
    first = 2 + 2 * count
    return pl.pallas_call(
        functools.partial(back_kernel, pieces, bits),
        out_shape=[
            jax.ShapeDtypeStruct((din, cols), F32),
            jax.ShapeDtypeStruct((1, din, cols), F32),
        ],
        in_specs=[VMEM] * first + [ANY] * len(kept),
        out_specs=[ANY] * 2,
        input_output_aliases={first + n: n for n in range(len(kept))},
        scratch_shapes=[
            pltpu.VMEM((count, din, width), F32),
            pltpu.VMEM((count, din, width), F32),
            pltpu.SemaphoreType.DMA((2 * count,)),
        ],
        compiler_params=pltpu.CompilerParams(vmem_limit_bytes=16 << 20),
    )(basis, wt, *rights, *merged, *kept)


def step(acts, out_grad, weight, error, start_q):
    replicas = lax.axis_size("dp")
    n_tensor = lax.axis_size("tensor")
    bits = [1 << b for b in range(1, replicas.bit_length() - 1)]
    pair = swap(1, 1, replicas)

    table, relays = rounds_of(n_tensor)
    acts_t, rows, blocks = blocks_of(acts, out_grad, weight, table)

    def across(block, n, only=range(n_tensor)):
        hops = [(a, to) for a, (to, _) in sorted(table[n].items()) if a in only]
        return lax.ppermute(block, "tensor", hops)

    received = [across(blocks[1], 0)]
    theirs, mine = merged_of(acts_t, error, rows)
    came = lax.ppermute(theirs, "dp", pair)
    left = left_of(start_q.T, theirs, mine)
    total, give = begin(mine, came, bits)
    came = lax.ppermute(give, "dp", swap(bits[0], bits[-1], replicas))
    left = left + lax.ppermute(left, "dp", swap(bits[-1], bits[0], replicas))
    for n, (one, other) in enumerate(zip(bits[1:], bits[-2::-1]), 2):
        total = total + came
        came = lax.ppermute(total, "dp", swap(one, other, replicas))
        left = left + lax.ppermute(left, "dp", swap(other, one, replicas))
    left_came = lax.ppermute(left, "dp", pair)

    for n in range(1, n_tensor - 1):
        block = blocks[n + 1]
        if relays and n == 1:
            between = (1, n_tensor - 2)
            ends = [a for a in range(n_tensor) if a not in between]
            received.append(across(block, n, ends))
            onward = functools.partial(onward_kernel, n_tensor)
            block = summed(onward, block, received[0])
            received.append(across(block, n, between))
        else:
            received.append(across(block, n))
    gather = functools.partial(gather_kernel, n_tensor if relays else None)
    input_grad = summed(gather, *received, blocks[0])

    basis = solve(left, left_came, replicas)
    right = right_of(left, left_came, total, came, replicas)
    beside = lax.ppermute(right, "dp", swap(bits[0], bits[-1], replicas))
    diagonal = lax.ppermute(right, "dp", swap(bits[0] | 1, bits[-1] | 1, replicas))
    across_pair = lax.ppermute(right, "dp", pair)
    pieces = ((True, True), (True, False), (False, True))
    rights = (right, beside, across_pair)
    kept = back(pieces, bits, basis, weight, rights, (mine, mine, theirs))
    new_weight, new_error = back(
        ((False, False),), bits, basis, weight, (diagonal,), (theirs,), *kept
    )
    return (new_weight, new_error, input_grad)


def solution(mesh):
    placed = (
        P("dp", None),
        P("dp", "tensor"),
        P(None, "tensor"),
        P("dp", None, "tensor"),
        P("tensor", None),
    )
    return jax.shard_map(
        step,
        mesh=mesh,
        in_specs=placed,
        out_specs=(P(None, "tensor"), P("dp", None, "tensor"), P(("dp", "tensor"), None)),
        check_vma=False,
    )
```

```python
import functools
import math

import jax
import jax.numpy as jnp
from jax import lax
from jax.experimental import pallas as pl
from jax.experimental.pallas import tpu as pltpu
from jax.sharding import PartitionSpec as P


F32 = jnp.float32
BF16 = jnp.bfloat16
NN = (((1,), (0,)), ((), ()))
NT = (((1,), (1,)), ((), ()))
VMEM_BYTES = 67043328
SPARE = 28 << 19
VMEM = pl.BlockSpec(memory_space=pltpu.VMEM)
ANY = pl.BlockSpec(memory_space=pl.ANY)
HBM = pl.BlockSpec(memory_space=pltpu.HBM)


def swap(bit_even, bit_odd, size):
    return [(i, i ^ (bit_odd if i & 1 else bit_even)) for i in range(size)]


def split(x):
    high = x.astype(BF16)
    return high, (x - high.astype(F32)).astype(BF16)


def dot(a, b, dims):
    return lax.dot_general(a, b, dims, preferred_element_type=F32)


def dot3(a, b, dims):
    (ah, al), (bh, bl) = split(a), split(b)
    return dot(ah, bh, dims) + (dot(ah, bl, dims) + dot(al, bh, dims))


def rounds_of(n):
    flows = sorted(
        ((a, b) for a in range(n) for b in range(n) if a != b),
        key=lambda flow: (abs(flow[0] - flow[1]), flow),
    )

    def fill(chosen, order):
        for a, b in list(flows)[::order]:
            if a not in chosen and all(b != to for to, _ in chosen.values()):
                chosen[a] = (b, b)
                flows.remove((a, b))
        return chosen

    relay, last = {}, {}
    if n >= 4:
        for gone in ((0, n - 2), (n - 1, 1), (1, n - 2), (n - 2, 1)):
            flows.remove(gone)
        relay = fill({0: (1, n - 2), n - 1: (n - 2, 1)}, -1)
        last = fill({1: (n - 2, n - 2), n - 2: (1, 1)}, -1)
    plain = []
    while flows:
        plain.append(fill({}, 1))
    rounds = [relay, last, *plain] if relay else plain
    if len(rounds) == n - 1 and all(len(one) == n for one in rounds):
        return rounds, bool(relay)
    return [{a: ((a + k) % n,) * 2 for a in range(n)} for k in range(1, n)], False


def pick(me, table, n):
    index = jnp.int32(0)
    for a in range(n):
        index = jnp.where(me == a, table[a][1] if a in table else a, index)
    return index


def part_of(rows, high, low):
    both = jnp.concatenate([high[...], low[...]], axis=1)
    return dot(jnp.concatenate([rows, rows], axis=1), both, NT)


def first_kernel(tables, n, chunks, acts, og, wt, acts_t, high_v, low_v, out, *rest):
    rows_v, (acts_v, wt_v, sems) = rest[:n], rest[n:]
    tok = acts.shape[0]
    _, cols = wt.shape
    block = tok // n
    width = cols // chunks
    me = lax.axis_index("tensor")
    places = [pl.multiple_of(pick(me, table, n) * block, block) for table in tables]

    def load(src, dst, at):
        copy = pltpu.make_async_copy(src, dst, sems.at[at])
        copy.start()
        return copy

    acts_in = [
        load(acts.at[pl.ds(at, block), :], acts_v.at[k * block : (k + 1) * block, :], k)
        for k, at in enumerate(places)
    ]
    wt_in = [
        load(wt.at[:, c * width : (c + 1) * width], wt_v.at[c], 2 * n + c) for c in range(chunks)
    ]
    rows_in = [load(og.at[pl.ds(at, block), :], rows_v[k], n + k) for k, at in enumerate(places)]
    for copy in acts_in:
        copy.wait()
    acts_t[...] = acts_v[...].T
    for c in range(chunks):
        wt_in[c].wait()
        high, low = split(wt_v[c])
        high_v[:, c * width : (c + 1) * width] = high
        low_v[:, c * width : (c + 1) * width] = low
    rows_in[0].wait()
    out[...] = part_of(rows_v[0][...], high_v, low_v)
    for copy in rows_in[1:]:
        copy.wait()


def first_of(acts, og, wt, tables):
    n = len(tables)
    tok = og.shape[0]
    din, cols = wt.shape
    chunks = 2
    block = tok // n
    shape = jax.ShapeDtypeStruct
    acts_t, high, low, out, *rows = pl.pallas_call(
        functools.partial(first_kernel, tables, n, chunks),
        out_shape=[
            shape((din, tok), BF16),
            shape((din, cols), BF16),
            shape((din, cols), BF16),
            shape((block, din), F32),
        ]
        + [shape((block, cols), BF16)] * n,
        in_specs=[HBM] * 3,
        out_specs=[VMEM] * (4 + n),
        scratch_shapes=[
            pltpu.VMEM((tok, din), BF16),
            pltpu.VMEM((chunks, din, cols // chunks), F32),
            pltpu.SemaphoreType.DMA((2 * n + chunks,)),
        ],
        compiler_params=pltpu.CompilerParams(vmem_limit_bytes=VMEM_BYTES - SPARE),
        cost_estimate=pl.CostEstimate(
            flops=4 * block * din * cols, bytes_accessed=4 << 20, transcendentals=0
        ),
        name="first",
    )(acts, og, wt)
    return acts_t, (high, low), out, rows


def rest_kernel(high, low, *rest):
    count = len(rest) // 2
    for rows, out in zip(rest[:count], rest[count:]):
        out[...] = part_of(rows[...], high, low)


def rest_of(halves, rows):
    block, cols = rows[0].shape
    din = halves[0].shape[0]
    return pl.pallas_call(
        rest_kernel,
        out_shape=[jax.ShapeDtypeStruct((block, din), F32)] * len(rows),
        in_specs=[VMEM] * (2 + len(rows)),
        out_specs=[VMEM] * len(rows),
        compiler_params=pltpu.CompilerParams(vmem_limit_bytes=12 << 20),
        cost_estimate=pl.CostEstimate(
            flops=4 * len(rows) * block * din * cols, bytes_accessed=4 << 20, transcendentals=0
        ),
        name="rest",
    )(*halves, *rows)


def merged_kernel(acts_t, err, *rest):
    rows, (theirs, mine) = rest[:-2], rest[-2:]
    tok = acts_t.shape[1]
    half = theirs.shape[1]
    side = lax.rem(lax.axis_index("dp"), 2)
    scale = 1.0 / math.sqrt(tok)
    for where, out in ((1 - side, theirs), (side, mine)):
        span = pl.ds(pl.multiple_of(where * half, half), half)
        columns = jnp.concatenate([one[:, span] for one in rows], axis=0)
        out[...] = dot(acts_t[...], columns, NN) * scale + err[0, :, span]


def merged_of(acts_t, err, rows):
    din, cols = err.shape[1:]
    tok = acts_t.shape[1]
    return pl.pallas_call(
        merged_kernel,
        out_shape=[jax.ShapeDtypeStruct((din, cols // 2), F32)] * 2,
        in_specs=[VMEM] * (2 + len(rows)),
        out_specs=[VMEM] * 2,
        compiler_params=pltpu.CompilerParams(vmem_limit_bytes=8 << 20),
        cost_estimate=pl.CostEstimate(
            flops=2 * tok * din * cols, bytes_accessed=4 << 20, transcendentals=0
        ),
        name="merged",
    )(acts_t, err, *rows)


def is_between(n_tensor):
    me = lax.axis_index("tensor")
    return ((me == 1) | (me == n_tensor - 2)).astype(F32)


def onward_kernel(n_tensor, block, relayed, out):
    out[...] = block[...] + is_between(n_tensor) * relayed[...]


def gather_kernel(relays, first, *rest):
    total = first[...]
    if relays:
        total = total * (1.0 - is_between(relays))
    for part in rest[:-1]:
        total = total + part[...]
    rest[-1][...] = total


def summed(kernel, *parts):
    return pl.pallas_call(
        kernel,
        out_shape=jax.ShapeDtypeStruct(parts[0].shape, F32),
        in_specs=[VMEM] * len(parts),
        out_specs=VMEM,
        compiler_params=pltpu.CompilerParams(vmem_limit_bytes=4 << 20),
    )(*parts)


def left_kernel(qt, theirs, mine, o_ref):
    half = theirs.shape[1]
    side = lax.rem(lax.axis_index("dp"), 2)
    far = qt[:, pl.ds(pl.multiple_of((1 - side) * half, half), half)]
    near = qt[:, pl.ds(pl.multiple_of(side * half, half), half)]
    o_ref[...] = dot3(far, theirs[...], NT) + dot3(near, mine[...], NT)


def left_of(qt, theirs, mine):
    return pl.pallas_call(
        left_kernel,
        out_shape=jax.ShapeDtypeStruct((qt.shape[0], mine.shape[0]), F32),
        in_specs=[VMEM] * 3,
        out_specs=VMEM,
        compiler_params=pltpu.CompilerParams(vmem_limit_bytes=8 << 20),
        name="left",
    )(qt, theirs, mine)


def solve_kernel(replicas, a_ref, b_ref, y_ref):
    left = (a_ref[...] + b_ref[...]) * (1.0 / replicas)
    rank, din = left.shape
    gram = lax.dot_general(
        left, left, NT, precision=lax.Precision.HIGHEST, preferred_element_type=F32
    )
    tiles, lanes = rank // 8, 128
    spans = range(0, din, lanes)
    state = [
        [gram[8 * i : 8 * i + 8, :]] + [left[8 * i : 8 * i + 8, at : at + lanes] for at in spans]
        for i in range(tiles)
    ]
    sub = lax.broadcasted_iota(jnp.int32, (8, lanes), 0)
    for k in range(0, rank, 2):
        i, s = divmod(k, 8)
        first = [jnp.broadcast_to(row[0][:, k : k + 1], (8, lanes)) for row in state]
        second = [jnp.broadcast_to(row[0][:, k + 1 : k + 2], (8, lanes)) for row in state]
        a = first[i][s : s + 1, :]
        b = second[i][s : s + 1, :]
        d = second[i][s + 1 : s + 2, :]
        inverse = 1.0 / (a * d - b * b)
        p, q, r = d * inverse, b * inverse, a * inverse
        for part in range(len(state[0])):
            wide = state[0][part].shape[1]
            top = state[i][part][s : s + 1, :]
            low = state[i][part][s + 1 : s + 2, :]
            new_top = p[:, :wide] * top - q[:, :wide] * low
            new_low = r[:, :wide] * low - q[:, :wide] * top
            for j in range(tiles):
                old = state[j][part]
                new = old - first[j][:, :wide] * new_top - second[j][:, :wide] * new_low
                if j == i:
                    new = jnp.where(sub[:, :wide] == s, new_top, new)
                    new = jnp.where(sub[:, :wide] == s + 1, new_low, new)
                state[j][part] = new
    for j in range(tiles):
        for n, at in enumerate(spans):
            y_ref[8 * j : 8 * j + 8, at : at + lanes] = state[j][1 + n]


def solve(a, b, replicas):
    return pl.pallas_call(
        functools.partial(solve_kernel, replicas),
        out_shape=jax.ShapeDtypeStruct(a.shape, F32),
        in_specs=[VMEM] * 2,
        out_specs=VMEM,
        compiler_params=pltpu.CompilerParams(vmem_limit_bytes=4 << 20),
        cost_estimate=pl.CostEstimate(
            flops=1 << 30, bytes_accessed=1 << 20, transcendentals=0
        ),
        name="solve",
    )(a, b)


def quarter(bits, side, index):
    even, odd = (lax.rem(index // bit, 2) for bit in (bits[0], bits[-1]))
    return jnp.where(side == 0, even, odd)


def begin_kernel(bits, mine, came, keep, give):
    width = keep.shape[1]
    index = lax.axis_index("dp")
    own = quarter(bits, lax.rem(index, 2), index)
    for which, out in ((own, keep), (1 - own, give)):
        span = pl.ds(pl.multiple_of(which * width, width), width)
        out[...] = mine[:, span] + came[:, span]


def begin(mine, came, bits):
    din, half = mine.shape
    return pl.pallas_call(
        functools.partial(begin_kernel, bits),
        out_shape=[jax.ShapeDtypeStruct((din, half // 2), F32)] * 2,
        in_specs=[VMEM] * 2,
        out_specs=[VMEM] * 2,
        compiler_params=pltpu.CompilerParams(vmem_limit_bytes=4 << 20),
        name="begin",
    )(mine, came)


def right_kernel(replicas, left_a, left_b, total_a, total_b, out):
    left = (left_a[...] + left_b[...]) * (1.0 / replicas)
    out[...] = dot3(left, (total_a[...] + total_b[...]) * (1.0 / replicas), NN)


def right_of(left, left_came, total, came, replicas):
    return pl.pallas_call(
        functools.partial(right_kernel, replicas),
        out_shape=jax.ShapeDtypeStruct((left.shape[0], total.shape[1]), F32),
        in_specs=[VMEM] * 4,
        out_specs=VMEM,
        compiler_params=pltpu.CompilerParams(vmem_limit_bytes=8 << 20),
        name="right",
    )(left, left_came, total, came)


def back_kernel(pieces, bits, basis, wt, *rest):
    count = len(pieces)
    rights, merged = rest[:count], rest[count : 2 * count]
    new_w, new_e, wv, ev, sems = rest[-5:]
    width = rights[0].shape[1]
    index = lax.axis_index("dp")
    flipped = basis[...].T
    copies = []
    for c, (near, same) in enumerate(pieces):
        side = lax.rem(index, 2)
        side = side if near else 1 - side
        own = quarter(bits, side, index)
        which = own if same else 1 - own
        here = pl.ds(pl.multiple_of(which * width, width), width)
        span = pl.ds(pl.multiple_of((2 * side + which) * width, width), width)
        delta = dot3(flipped, rights[c][...], NN)
        ev[c] = merged[c][:, here] - delta
        wv[c] = wt[:, span] - delta
        for one in (
            pltpu.make_async_copy(ev.at[c], new_e.at[0, :, span], sems.at[2 * c]),
            pltpu.make_async_copy(wv.at[c], new_w.at[:, span], sems.at[2 * c + 1]),
        ):
            one.start()
            copies.append(one)
    for one in copies:
        one.wait()


def back(pieces, bits, basis, wt, rights, merged, *kept):
    din, cols = wt.shape
    count = len(pieces)
    width = rights[0].shape[1]
    first = 2 + 2 * count
    return pl.pallas_call(
        functools.partial(back_kernel, pieces, bits),
        out_shape=[
            jax.ShapeDtypeStruct((din, cols), F32),
            jax.ShapeDtypeStruct((1, din, cols), F32),
        ],
        in_specs=[VMEM] * first + [ANY] * len(kept),
        out_specs=[ANY] * 2,
        input_output_aliases={first + n: n for n in range(len(kept))},
        scratch_shapes=[
            pltpu.VMEM((count, din, width), F32),
            pltpu.VMEM((count, din, width), F32),
            pltpu.SemaphoreType.DMA((2 * count,)),
        ],
        compiler_params=pltpu.CompilerParams(vmem_limit_bytes=16 << 20),
    )(basis, wt, *rights, *merged, *kept)


def send(x, axis, pairs):
    return lax.ppermute(x, axis, pairs)


def step(acts, out_grad, weight, error, start_q):
    replicas = lax.axis_size("dp")
    n_tensor = lax.axis_size("tensor")
    bits = [1 << b for b in range(1, replicas.bit_length() - 1)]
    pair = swap(1, 1, replicas)

    table, relays = rounds_of(n_tensor)
    tables = [table[0], {}, *table[1:]]
    acts_t, halves, first, rows = first_of(acts, out_grad, weight, tables)

    def across(block, n):
        return send(block, "tensor", [(a, to) for a, (to, _) in sorted(table[n].items())])

    received = [across(first, 0)]
    theirs, mine = merged_of(acts_t, error, rows)
    came = send(theirs, "dp", pair)
    left = left_of(start_q.T, theirs, mine)
    total, give = begin(mine, came, bits)
    came = send(give, "dp", swap(bits[0], bits[-1], replicas))
    left = left + send(left, "dp", swap(bits[-1], bits[0], replicas))
    for n, (one, other) in enumerate(zip(bits[1:], bits[-2::-1]), 2):
        total = total + came
        came = send(total, "dp", swap(one, other, replicas))
        left = left + send(left, "dp", swap(other, one, replicas))
    left_came = send(left, "dp", pair)

    blocks = rest_of(halves, rows[1:])
    for n in range(1, n_tensor - 1):
        block = blocks[n]
        if relays and n == 1:
            onward = functools.partial(onward_kernel, n_tensor)
            block = summed(onward, block, received[0])
        received.append(across(block, n))
    gather = functools.partial(gather_kernel, n_tensor if relays else None)
    input_grad = summed(gather, *received, blocks[0])

    basis = solve(left, left_came, replicas)
    right = right_of(left, left_came, total, came, replicas)
    beside = send(right, "dp", swap(bits[0], bits[-1], replicas))
    diagonal = send(right, "dp", swap(bits[0] | 1, bits[-1] | 1, replicas))
    across_pair = send(right, "dp", pair)
    pieces = ((True, True), (True, False), (False, True))
    rights = (right, beside, across_pair)
    kept = back(pieces, bits, basis, weight, rights, (mine, mine, theirs))
    new_weight, new_error = back(
        ((False, False),), bits, basis, weight, (diagonal,), (theirs,), *kept
    )
    return (new_weight, new_error, input_grad)


def solution(mesh):
    placed = (
        P("dp", None),
        P("dp", "tensor"),
        P(None, "tensor"),
        P("dp", None, "tensor"),
        P("tensor", None),
    )
    return jax.shard_map(
        step,
        mesh=mesh,
        in_specs=placed,
        out_specs=(P(None, "tensor"), P("dp", None, "tensor"), P(("dp", "tensor"), None)),
        check_vma=False,
    )
```

```python
import functools
import math

import jax
import jax.numpy as jnp
from jax import lax
from jax.experimental import pallas as pl
from jax.experimental.pallas import tpu as pltpu
from jax.sharding import PartitionSpec as P


F32 = jnp.float32
BF16 = jnp.bfloat16
NN = (((1,), (0,)), ((), ()))
NT = (((1,), (1,)), ((), ()))
VMEM_BYTES = 67043328
SPARE = 28 << 19
VMEM = pl.BlockSpec(memory_space=pltpu.VMEM)
ANY = pl.BlockSpec(memory_space=pl.ANY)
HBM = pl.BlockSpec(memory_space=pltpu.HBM)


def swap(bit_even, bit_odd, size):
    return [(i, i ^ (bit_odd if i & 1 else bit_even)) for i in range(size)]


def split(x):
    high = x.astype(BF16)
    return high, (x - high.astype(F32)).astype(BF16)


def dot(a, b, dims):
    return lax.dot_general(a, b, dims, preferred_element_type=F32)


def dot3(a, b, dims):
    (ah, al), (bh, bl) = split(a), split(b)
    return dot(ah, bh, dims) + (dot(ah, bl, dims) + dot(al, bh, dims))


def rounds_of(n):
    flows = sorted(
        ((a, b) for a in range(n) for b in range(n) if a != b),
        key=lambda flow: (abs(flow[0] - flow[1]), flow),
    )

    def fill(chosen, order):
        for a, b in list(flows)[::order]:
            if a not in chosen and all(b != to for to, _ in chosen.values()):
                chosen[a] = (b, b)
                flows.remove((a, b))
        return chosen

    relay, last = {}, {}
    if n >= 4:
        for gone in ((0, n - 2), (n - 1, 1), (1, n - 2), (n - 2, 1)):
            flows.remove(gone)
        relay = fill({0: (1, n - 2), n - 1: (n - 2, 1)}, -1)
        last = fill({1: (n - 2, n - 2), n - 2: (1, 1)}, -1)
    plain = []
    while flows:
        plain.append(fill({}, 1))
    rounds = [relay, last, *plain] if relay else plain
    if len(rounds) == n - 1 and all(len(one) == n for one in rounds):
        return rounds, bool(relay)
    return [{a: ((a + k) % n,) * 2 for a in range(n)} for k in range(1, n)], False


def pick(me, table, n):
    index = jnp.int32(0)
    for a in range(n):
        index = jnp.where(me == a, table[a][1] if a in table else a, index)
    return index


def part_of(rows, high, low):
    both = jnp.concatenate([high[...], low[...]], axis=1)
    return dot(jnp.concatenate([rows, rows], axis=1), both, NT)


def first_kernel(tables, n, chunks, acts, og, wt, acts_t, high_v, low_v, out, *rest):
    rows_v, (acts_v, wt_v, sems) = rest[:n], rest[n:]
    tok = acts.shape[0]
    _, cols = wt.shape
    block = tok // n
    width = cols // chunks
    me = lax.axis_index("tensor")
    places = [pl.multiple_of(pick(me, table, n) * block, block) for table in tables]

    def load(src, dst, at):
        copy = pltpu.make_async_copy(src, dst, sems.at[at])
        copy.start()
        return copy

    acts_in = [
        load(acts.at[pl.ds(at, block), :], acts_v.at[k * block : (k + 1) * block, :], k)
        for k, at in enumerate(places)
    ]
    wt_in = [
        load(wt.at[:, c * width : (c + 1) * width], wt_v.at[c], 2 * n + c) for c in range(chunks)
    ]
    rows_in = [load(og.at[pl.ds(at, block), :], rows_v[k], n + k) for k, at in enumerate(places)]
    for copy in acts_in:
        copy.wait()
    acts_t[...] = acts_v[...].T
    for c in range(chunks):
        wt_in[c].wait()
        high, low = split(wt_v[c])
        high_v[:, c * width : (c + 1) * width] = high
        low_v[:, c * width : (c + 1) * width] = low
    rows_in[0].wait()
    out[...] = part_of(rows_v[0][...], high_v, low_v)
    for copy in rows_in[1:]:
        copy.wait()


def first_of(acts, og, wt, tables):
    n = len(tables)
    tok = og.shape[0]
    din, cols = wt.shape
    chunks = 2
    block = tok // n
    shape = jax.ShapeDtypeStruct
    acts_t, high, low, out, *rows = pl.pallas_call(
        functools.partial(first_kernel, tables, n, chunks),
        out_shape=[
            shape((din, tok), BF16),
            shape((din, cols), BF16),
            shape((din, cols), BF16),
            shape((block, din), F32),
        ]
        + [shape((block, cols), BF16)] * n,
        in_specs=[HBM] * 3,
        out_specs=[VMEM] * (4 + n),
        scratch_shapes=[
            pltpu.VMEM((tok, din), BF16),
            pltpu.VMEM((chunks, din, cols // chunks), F32),
            pltpu.SemaphoreType.DMA((2 * n + chunks,)),
        ],
        compiler_params=pltpu.CompilerParams(vmem_limit_bytes=VMEM_BYTES - SPARE),
        cost_estimate=pl.CostEstimate(
            flops=4 * block * din * cols, bytes_accessed=4 << 20, transcendentals=0
        ),
        name="first",
    )(acts, og, wt)
    return acts_t, (high, low), out, rows


def rest_kernel(high, low, *rest):
    count = len(rest) // 2
    for rows, out in zip(rest[:count], rest[count:]):
        out[...] = part_of(rows[...], high, low)


def rest_of(halves, rows):
    block, cols = rows[0].shape
    din = halves[0].shape[0]
    return pl.pallas_call(
        rest_kernel,
        out_shape=[jax.ShapeDtypeStruct((block, din), F32)] * len(rows),
        in_specs=[VMEM] * (2 + len(rows)),
        out_specs=[VMEM] * len(rows),
        compiler_params=pltpu.CompilerParams(vmem_limit_bytes=12 << 20),
        cost_estimate=pl.CostEstimate(
            flops=4 * len(rows) * block * din * cols, bytes_accessed=4 << 20, transcendentals=0
        ),
        name="rest",
    )(*halves, *rows)


def merged_kernel(acts_t, err, *rest):
    rows, (theirs, mine) = rest[:-2], rest[-2:]
    tok = acts_t.shape[1]
    half = theirs.shape[1]
    side = lax.rem(lax.axis_index("dp"), 2)
    scale = 1.0 / math.sqrt(tok)
    for where, out in ((1 - side, theirs), (side, mine)):
        span = pl.ds(pl.multiple_of(where * half, half), half)
        columns = jnp.concatenate([one[:, span] for one in rows], axis=0)
        out[...] = dot(acts_t[...], columns, NN) * scale + err[0, :, span]


def merged_of(acts_t, err, rows):
    din, cols = err.shape[1:]
    tok = acts_t.shape[1]
    return pl.pallas_call(
        merged_kernel,
        out_shape=[jax.ShapeDtypeStruct((din, cols // 2), F32)] * 2,
        in_specs=[VMEM] * (2 + len(rows)),
        out_specs=[VMEM] * 2,
        compiler_params=pltpu.CompilerParams(vmem_limit_bytes=8 << 20),
        cost_estimate=pl.CostEstimate(
            flops=2 * tok * din * cols, bytes_accessed=4 << 20, transcendentals=0
        ),
        name="merged",
    )(acts_t, err, *rows)


def is_between(n_tensor):
    me = lax.axis_index("tensor")
    return ((me == 1) | (me == n_tensor - 2)).astype(F32)


def onward_kernel(n_tensor, block, relayed, out):
    out[...] = block[...] + is_between(n_tensor) * relayed[...]


def gather_kernel(relays, first, *rest):
    total = first[...]
    if relays:
        total = total * (1.0 - is_between(relays))
    for part in rest[:-1]:
        total = total + part[...]
    rest[-1][...] = total


def summed(kernel, *parts):
    return pl.pallas_call(
        kernel,
        out_shape=jax.ShapeDtypeStruct(parts[0].shape, F32),
        in_specs=[VMEM] * len(parts),
        out_specs=VMEM,
        compiler_params=pltpu.CompilerParams(vmem_limit_bytes=4 << 20),
    )(*parts)


def left_kernel(qt, theirs, mine, o_ref):
    half = theirs.shape[1]
    side = lax.rem(lax.axis_index("dp"), 2)
    far = qt[:, pl.ds(pl.multiple_of((1 - side) * half, half), half)]
    near = qt[:, pl.ds(pl.multiple_of(side * half, half), half)]
    o_ref[...] = dot3(far, theirs[...], NT) + dot3(near, mine[...], NT)


def left_of(qt, theirs, mine):
    return pl.pallas_call(
        left_kernel,
        out_shape=jax.ShapeDtypeStruct((qt.shape[0], mine.shape[0]), F32),
        in_specs=[VMEM] * 3,
        out_specs=VMEM,
        compiler_params=pltpu.CompilerParams(vmem_limit_bytes=8 << 20),
        name="left",
    )(qt, theirs, mine)


def solve_kernel(replicas, a_ref, b_ref, y_ref):
    left = (a_ref[...] + b_ref[...]) * (1.0 / replicas)
    rank, din = left.shape
    gram = lax.dot_general(
        left, left, NT, precision=lax.Precision.HIGHEST, preferred_element_type=F32
    )
    tiles, lanes = rank // 8, 128
    spans = range(0, din, lanes)
    state = [
        [gram[8 * i : 8 * i + 8, :]] + [left[8 * i : 8 * i + 8, at : at + lanes] for at in spans]
        for i in range(tiles)
    ]
    sub = lax.broadcasted_iota(jnp.int32, (8, lanes), 0)
    for k in range(0, rank, 2):
        i, s = divmod(k, 8)
        first = [jnp.broadcast_to(row[0][:, k : k + 1], (8, lanes)) for row in state]
        second = [jnp.broadcast_to(row[0][:, k + 1 : k + 2], (8, lanes)) for row in state]
        a = first[i][s : s + 1, :]
        b = second[i][s : s + 1, :]
        d = second[i][s + 1 : s + 2, :]
        inverse = 1.0 / (a * d - b * b)
        p, q, r = d * inverse, b * inverse, a * inverse
        for part in range(len(state[0])):
            wide = state[0][part].shape[1]
            top = state[i][part][s : s + 1, :]
            low = state[i][part][s + 1 : s + 2, :]
            new_top = p[:, :wide] * top - q[:, :wide] * low
            new_low = r[:, :wide] * low - q[:, :wide] * top
            for j in range(tiles):
                old = state[j][part]
                new = old - first[j][:, :wide] * new_top - second[j][:, :wide] * new_low
                if j == i:
                    new = jnp.where(sub[:, :wide] == s, new_top, new)
                    new = jnp.where(sub[:, :wide] == s + 1, new_low, new)
                state[j][part] = new
    for j in range(tiles):
        for n, at in enumerate(spans):
            y_ref[8 * j : 8 * j + 8, at : at + lanes] = state[j][1 + n]


def solve(a, b, replicas):
    return pl.pallas_call(
        functools.partial(solve_kernel, replicas),
        out_shape=jax.ShapeDtypeStruct(a.shape, F32),
        in_specs=[VMEM] * 2,
        out_specs=VMEM,
        compiler_params=pltpu.CompilerParams(vmem_limit_bytes=4 << 20),
        cost_estimate=pl.CostEstimate(
            flops=1 << 30, bytes_accessed=1 << 20, transcendentals=0
        ),
        name="solve",
    )(a, b)


def quarter(bits, side, index):
    even, odd = (lax.rem(index // bit, 2) for bit in (bits[0], bits[-1]))
    return jnp.where(side == 0, even, odd)


def begin_kernel(bits, mine, came, keep, give):
    width = keep.shape[1]
    index = lax.axis_index("dp")
    own = quarter(bits, lax.rem(index, 2), index)
    for which, out in ((own, keep), (1 - own, give)):
        span = pl.ds(pl.multiple_of(which * width, width), width)
        out[...] = mine[:, span] + came[:, span]


def begin(mine, came, bits):
    din, half = mine.shape
    return pl.pallas_call(
        functools.partial(begin_kernel, bits),
        out_shape=[jax.ShapeDtypeStruct((din, half // 2), F32)] * 2,
        in_specs=[VMEM] * 2,
        out_specs=[VMEM] * 2,
        compiler_params=pltpu.CompilerParams(vmem_limit_bytes=4 << 20),
        name="begin",
    )(mine, came)


def right_kernel(replicas, left_a, left_b, total_a, total_b, out):
    left = (left_a[...] + left_b[...]) * (1.0 / replicas)
    out[...] = dot3(left, (total_a[...] + total_b[...]) * (1.0 / replicas), NN)


def right_of(left, left_came, total, came, replicas):
    return pl.pallas_call(
        functools.partial(right_kernel, replicas),
        out_shape=jax.ShapeDtypeStruct((left.shape[0], total.shape[1]), F32),
        in_specs=[VMEM] * 4,
        out_specs=VMEM,
        compiler_params=pltpu.CompilerParams(vmem_limit_bytes=8 << 20),
        name="right",
    )(left, left_came, total, came)


def back_kernel(pieces, bits, basis, wt, *rest):
    count = len(pieces)
    rights, merged = rest[:count], rest[count : 2 * count]
    new_w, new_e, wv, ev, sems = rest[-5:]
    width = rights[0].shape[1]
    index = lax.axis_index("dp")
    flipped = basis[...].T
    copies = []
    for c, (near, same) in enumerate(pieces):
        side = lax.rem(index, 2)
        side = side if near else 1 - side
        own = quarter(bits, side, index)
        which = own if same else 1 - own
        here = pl.ds(pl.multiple_of(which * width, width), width)
        span = pl.ds(pl.multiple_of((2 * side + which) * width, width), width)
        delta = dot3(flipped, rights[c][...], NN)
        ev[c] = merged[c][:, here] - delta
        wv[c] = wt[:, span] - delta
        for one in (
            pltpu.make_async_copy(ev.at[c], new_e.at[0, :, span], sems.at[2 * c]),
            pltpu.make_async_copy(wv.at[c], new_w.at[:, span], sems.at[2 * c + 1]),
        ):
            one.start()
            copies.append(one)
    for one in copies:
        one.wait()


def back(pieces, bits, basis, wt, rights, merged, *kept):
    din, cols = wt.shape
    count = len(pieces)
    width = rights[0].shape[1]
    first = 2 + 2 * count
    return pl.pallas_call(
        functools.partial(back_kernel, pieces, bits),
        out_shape=[
            jax.ShapeDtypeStruct((din, cols), F32),
            jax.ShapeDtypeStruct((1, din, cols), F32),
        ],
        in_specs=[VMEM] * first + [ANY] * len(kept),
        out_specs=[ANY] * 2,
        input_output_aliases={first + n: n for n in range(len(kept))},
        scratch_shapes=[
            pltpu.VMEM((count, din, width), F32),
            pltpu.VMEM((count, din, width), F32),
            pltpu.SemaphoreType.DMA((2 * count,)),
        ],
        compiler_params=pltpu.CompilerParams(vmem_limit_bytes=16 << 20),
    )(basis, wt, *rights, *merged, *kept)


def step(acts, out_grad, weight, error, start_q):
    replicas = lax.axis_size("dp")
    n_tensor = lax.axis_size("tensor")
    bits = [1 << b for b in range(1, replicas.bit_length() - 1)]
    pair = swap(1, 1, replicas)

    table, relays = rounds_of(n_tensor)
    tables = [table[0], {}, *table[1:]]
    acts_t, halves, first, rows = first_of(acts, out_grad, weight, tables)

    def across(block, n, only=range(n_tensor)):
        hops = [(a, to) for a, (to, _) in sorted(table[n].items()) if a in only]
        return lax.ppermute(block, "tensor", hops)

    received = [across(first, 0)]
    theirs, mine = merged_of(acts_t, error, rows)
    came = lax.ppermute(theirs, "dp", pair)
    left = left_of(start_q.T, theirs, mine)
    total, give = begin(mine, came, bits)
    came = lax.ppermute(give, "dp", swap(bits[0], bits[-1], replicas))
    left = left + lax.ppermute(left, "dp", swap(bits[-1], bits[0], replicas))
    for n, (one, other) in enumerate(zip(bits[1:], bits[-2::-1]), 2):
        total = total + came
        came = lax.ppermute(total, "dp", swap(one, other, replicas))
        left = left + lax.ppermute(left, "dp", swap(other, one, replicas))
    left_came = lax.ppermute(left, "dp", pair)

    blocks = rest_of(halves, rows[1:])
    for n in range(1, n_tensor - 1):
        block = blocks[n]
        if relays and n == 1:
            between = (1, n_tensor - 2)
            ends = [a for a in range(n_tensor) if a not in between]
            received.append(across(block, n, ends))
            onward = functools.partial(onward_kernel, n_tensor)
            block = summed(onward, block, received[0])
            received.append(across(block, n, between))
        else:
            received.append(across(block, n))
    gather = functools.partial(gather_kernel, n_tensor if relays else None)
    input_grad = summed(gather, *received, blocks[0])

    basis = solve(left, left_came, replicas)
    right = right_of(left, left_came, total, came, replicas)
    across_pair = lax.ppermute(right, "dp", pair)
    beside = lax.ppermute(right, "dp", swap(bits[0], bits[-1], replicas))
    diagonal = lax.ppermute(right, "dp", swap(bits[0] | 1, bits[-1] | 1, replicas))
    halves = (mine, theirs)
    rights = (right, across_pair)
    kept = back(((True, True), (False, True)), bits, basis, weight, rights, halves)
    pieces, rights = ((True, False), (False, False)), (beside, diagonal)
    new_weight, new_error = back(pieces, bits, basis, weight, rights, halves, *kept)
    return (new_weight, new_error, input_grad)


def solution(mesh):
    placed = (
        P("dp", None),
        P("dp", "tensor"),
        P(None, "tensor"),
        P("dp", None, "tensor"),
        P("tensor", None),
    )
    return jax.shard_map(
        step,
        mesh=mesh,
        in_specs=placed,
        out_specs=(P(None, "tensor"), P("dp", None, "tensor"), P(("dp", "tensor"), None)),
        check_vma=False,
    )
```

```python
import functools
import math

import jax
import jax.numpy as jnp
from jax import lax
from jax.experimental import pallas as pl
from jax.experimental.pallas import tpu as pltpu
from jax.sharding import PartitionSpec as P


F32 = jnp.float32
BF16 = jnp.bfloat16
NN = (((1,), (0,)), ((), ()))
NT = (((1,), (1,)), ((), ()))
VMEM_BYTES = 67043328
SPARE = 28 << 19
VMEM = pl.BlockSpec(memory_space=pltpu.VMEM)
ANY = pl.BlockSpec(memory_space=pl.ANY)
HBM = pl.BlockSpec(memory_space=pltpu.HBM)


def swap(bit_even, bit_odd, size):
    return [(i, i ^ (bit_odd if i & 1 else bit_even)) for i in range(size)]


def split(x):
    high = x.astype(BF16)
    return high, (x - high.astype(F32)).astype(BF16)


def dot(a, b, dims):
    return lax.dot_general(a, b, dims, preferred_element_type=F32)


def dot3(a, b, dims):
    (ah, al), (bh, bl) = split(a), split(b)
    return dot(ah, bh, dims) + (dot(ah, bl, dims) + dot(al, bh, dims))


def rounds_of(n):
    if n % 2:
        return [({a: ((a + k) % n,) * 2 for a in range(n)}, None) for k in range(1, n)]
    pairs = n // 2

    def member(a, k, parity):
        return 2 * ((a // 2 + k) % pairs) + parity

    give = [
        ({a: (a ^ 1, member(a, k, 1 - a % 2)) for a in range(n)}, None) for k in range(1, pairs)
    ]
    onward = [
        ({a: (member(a, k, a % 2),) * 2 for a in range(n)}, k - 1) for k in range(1, pairs)
    ]
    return [*give, *onward, ({a: (a ^ 1, a ^ 1) for a in range(n)}, None)]


def pick(me, table, n):
    index = jnp.int32(0)
    for a in range(n):
        index = jnp.where(me == a, table[a][1] if table else a, index)
    return index


def part_of(rows, high, low):
    both = jnp.concatenate([high[...], low[...]], axis=1)
    return dot(jnp.concatenate([rows, rows], axis=1), both, NT)


def first_kernel(tables, n, chunks, acts, og, wt, acts_t, high_v, low_v, out, *rest):
    rows_v, (acts_v, wt_v, sems) = rest[:n], rest[n:]
    tok = acts.shape[0]
    _, cols = wt.shape
    block = tok // n
    width = cols // chunks
    me = lax.axis_index("tensor")
    places = [pl.multiple_of(pick(me, table, n) * block, block) for table in tables]

    def load(src, dst, at):
        copy = pltpu.make_async_copy(src, dst, sems.at[at])
        copy.start()
        return copy

    acts_in = [
        load(acts.at[pl.ds(at, block), :], acts_v.at[k * block : (k + 1) * block, :], k)
        for k, at in enumerate(places)
    ]
    wt_in = [
        load(wt.at[:, c * width : (c + 1) * width], wt_v.at[c], 2 * n + c) for c in range(chunks)
    ]
    rows_in = [load(og.at[pl.ds(at, block), :], rows_v[k], n + k) for k, at in enumerate(places)]
    for copy in acts_in:
        copy.wait()
    acts_t[...] = acts_v[...].T
    for c in range(chunks):
        wt_in[c].wait()
        high, low = split(wt_v[c])
        high_v[:, c * width : (c + 1) * width] = high
        low_v[:, c * width : (c + 1) * width] = low
    rows_in[0].wait()
    out[...] = part_of(rows_v[0][...], high_v, low_v)
    for copy in rows_in[1:]:
        copy.wait()


def first_of(acts, og, wt, tables):
    n = len(tables)
    tok = og.shape[0]
    din, cols = wt.shape
    chunks = 2
    block = tok // n
    shape = jax.ShapeDtypeStruct
    acts_t, high, low, out, *rows = pl.pallas_call(
        functools.partial(first_kernel, tables, n, chunks),
        out_shape=[
            shape((din, tok), BF16),
            shape((din, cols), BF16),
            shape((din, cols), BF16),
            shape((block, din), F32),
        ]
        + [shape((block, cols), BF16)] * n,
        in_specs=[HBM] * 3,
        out_specs=[VMEM] * (4 + n),
        scratch_shapes=[
            pltpu.VMEM((tok, din), BF16),
            pltpu.VMEM((chunks, din, cols // chunks), F32),
            pltpu.SemaphoreType.DMA((2 * n + chunks,)),
        ],
        compiler_params=pltpu.CompilerParams(vmem_limit_bytes=VMEM_BYTES - SPARE),
        cost_estimate=pl.CostEstimate(
            flops=4 * block * din * cols, bytes_accessed=4 << 20, transcendentals=0
        ),
        name="first",
    )(acts, og, wt)
    return acts_t, (high, low), out, rows


def rest_kernel(high, low, *rest):
    count = len(rest) // 2
    for rows, out in zip(rest[:count], rest[count:]):
        out[...] = part_of(rows[...], high, low)


def rest_of(halves, rows):
    block, cols = rows[0].shape
    din = halves[0].shape[0]
    return pl.pallas_call(
        rest_kernel,
        out_shape=[jax.ShapeDtypeStruct((block, din), F32)] * len(rows),
        in_specs=[VMEM] * (2 + len(rows)),
        out_specs=[VMEM] * len(rows),
        compiler_params=pltpu.CompilerParams(vmem_limit_bytes=12 << 20),
        cost_estimate=pl.CostEstimate(
            flops=4 * len(rows) * block * din * cols, bytes_accessed=4 << 20, transcendentals=0
        ),
        name="rest",
    )(*halves, *rows)


def merged_kernel(acts_t, err, *rest):
    rows, (theirs, mine) = rest[:-2], rest[-2:]
    tok = acts_t.shape[1]
    half = theirs.shape[1]
    side = lax.rem(lax.axis_index("dp"), 2)
    scale = 1.0 / math.sqrt(tok)
    for where, out in ((1 - side, theirs), (side, mine)):
        span = pl.ds(pl.multiple_of(where * half, half), half)
        columns = jnp.concatenate([one[:, span] for one in rows], axis=0)
        out[...] = dot(acts_t[...], columns, NN) * scale + err[0, :, span]


def merged_of(acts_t, err, rows):
    din, cols = err.shape[1:]
    tok = acts_t.shape[1]
    return pl.pallas_call(
        merged_kernel,
        out_shape=[jax.ShapeDtypeStruct((din, cols // 2), F32)] * 2,
        in_specs=[VMEM] * (2 + len(rows)),
        out_specs=[VMEM] * 2,
        compiler_params=pltpu.CompilerParams(vmem_limit_bytes=8 << 20),
        cost_estimate=pl.CostEstimate(
            flops=2 * tok * din * cols, bytes_accessed=4 << 20, transcendentals=0
        ),
        name="merged",
    )(acts_t, err, *rows)


def sum_kernel(*refs):
    total = refs[0][...]
    for part in refs[1:-1]:
        total = total + part[...]
    refs[-1][...] = total


def summed(*parts):
    return pl.pallas_call(
        sum_kernel,
        out_shape=jax.ShapeDtypeStruct(parts[0].shape, F32),
        in_specs=[VMEM] * len(parts),
        out_specs=VMEM,
        compiler_params=pltpu.CompilerParams(vmem_limit_bytes=4 << 20),
    )(*parts)


def left_kernel(qt, theirs, mine, o_ref):
    half = theirs.shape[1]
    side = lax.rem(lax.axis_index("dp"), 2)
    far = qt[:, pl.ds(pl.multiple_of((1 - side) * half, half), half)]
    near = qt[:, pl.ds(pl.multiple_of(side * half, half), half)]
    o_ref[...] = dot3(far, theirs[...], NT) + dot3(near, mine[...], NT)


def left_of(qt, theirs, mine):
    return pl.pallas_call(
        left_kernel,
        out_shape=jax.ShapeDtypeStruct((qt.shape[0], mine.shape[0]), F32),
        in_specs=[VMEM] * 3,
        out_specs=VMEM,
        compiler_params=pltpu.CompilerParams(vmem_limit_bytes=8 << 20),
        name="left",
    )(qt, theirs, mine)


def solve_kernel(replicas, a_ref, b_ref, y_ref):
    left = (a_ref[...] + b_ref[...]) * (1.0 / replicas)
    rank, din = left.shape
    gram = lax.dot_general(
        left, left, NT, precision=lax.Precision.HIGHEST, preferred_element_type=F32
    )
    tiles, lanes = rank // 8, 128
    spans = range(0, din, lanes)
    state = [
        [gram[8 * i : 8 * i + 8, :]] + [left[8 * i : 8 * i + 8, at : at + lanes] for at in spans]
        for i in range(tiles)
    ]
    sub = lax.broadcasted_iota(jnp.int32, (8, lanes), 0)
    for k in range(0, rank, 2):
        i, s = divmod(k, 8)
        first = [jnp.broadcast_to(row[0][:, k : k + 1], (8, lanes)) for row in state]
        second = [jnp.broadcast_to(row[0][:, k + 1 : k + 2], (8, lanes)) for row in state]
        a = first[i][s : s + 1, :]
        b = second[i][s : s + 1, :]
        d = second[i][s + 1 : s + 2, :]
        inverse = 1.0 / (a * d - b * b)
        p, q, r = d * inverse, b * inverse, a * inverse
        for part in range(len(state[0])):
            wide = state[0][part].shape[1]
            top = state[i][part][s : s + 1, :]
            low = state[i][part][s + 1 : s + 2, :]
            new_top = p[:, :wide] * top - q[:, :wide] * low
            new_low = r[:, :wide] * low - q[:, :wide] * top
            for j in range(tiles):
                old = state[j][part]
                new = old - first[j][:, :wide] * new_top - second[j][:, :wide] * new_low
                if j == i:
                    new = jnp.where(sub[:, :wide] == s, new_top, new)
                    new = jnp.where(sub[:, :wide] == s + 1, new_low, new)
                state[j][part] = new
    for j in range(tiles):
        for n, at in enumerate(spans):
            y_ref[8 * j : 8 * j + 8, at : at + lanes] = state[j][1 + n]


def solve(a, b, replicas):
    return pl.pallas_call(
        functools.partial(solve_kernel, replicas),
        out_shape=jax.ShapeDtypeStruct(a.shape, F32),
        in_specs=[VMEM] * 2,
        out_specs=VMEM,
        compiler_params=pltpu.CompilerParams(vmem_limit_bytes=4 << 20),
        cost_estimate=pl.CostEstimate(
            flops=1 << 30, bytes_accessed=1 << 20, transcendentals=0
        ),
        name="solve",
    )(a, b)


def quarter(bits, side, index):
    even, odd = (lax.rem(index // bit, 2) for bit in (bits[0], bits[-1]))
    return jnp.where(side == 0, even, odd)


def begin_kernel(bits, mine, came, keep, give):
    width = keep.shape[1]
    index = lax.axis_index("dp")
    own = quarter(bits, lax.rem(index, 2), index)
    for which, out in ((own, keep), (1 - own, give)):
        span = pl.ds(pl.multiple_of(which * width, width), width)
        out[...] = mine[:, span] + came[:, span]


def begin(mine, came, bits):
    din, half = mine.shape
    return pl.pallas_call(
        functools.partial(begin_kernel, bits),
        out_shape=[jax.ShapeDtypeStruct((din, half // 2), F32)] * 2,
        in_specs=[VMEM] * 2,
        out_specs=[VMEM] * 2,
        compiler_params=pltpu.CompilerParams(vmem_limit_bytes=4 << 20),
        name="begin",
    )(mine, came)


def right_kernel(replicas, left_a, left_b, total_a, total_b, out):
    left = (left_a[...] + left_b[...]) * (1.0 / replicas)
    out[...] = dot3(left, (total_a[...] + total_b[...]) * (1.0 / replicas), NN)


def right_of(left, left_came, total, came, replicas):
    return pl.pallas_call(
        functools.partial(right_kernel, replicas),
        out_shape=jax.ShapeDtypeStruct((left.shape[0], total.shape[1]), F32),
        in_specs=[VMEM] * 4,
        out_specs=VMEM,
        compiler_params=pltpu.CompilerParams(vmem_limit_bytes=8 << 20),
        name="right",
    )(left, left_came, total, came)


def back_kernel(pieces, bits, basis, wt, *rest):
    count = len(pieces)
    rights, merged = rest[:count], rest[count : 2 * count]
    new_w, new_e, wv, ev, sems = rest[-5:]
    width = rights[0].shape[1]
    index = lax.axis_index("dp")
    flipped = basis[...].T
    copies = []
    for c, (near, same) in enumerate(pieces):
        side = lax.rem(index, 2)
        side = side if near else 1 - side
        own = quarter(bits, side, index)
        which = own if same else 1 - own
        here = pl.ds(pl.multiple_of(which * width, width), width)
        span = pl.ds(pl.multiple_of((2 * side + which) * width, width), width)
        delta = dot3(flipped, rights[c][...], NN)
        ev[c] = merged[c][:, here] - delta
        wv[c] = wt[:, span] - delta
        for one in (
            pltpu.make_async_copy(ev.at[c], new_e.at[0, :, span], sems.at[2 * c]),
            pltpu.make_async_copy(wv.at[c], new_w.at[:, span], sems.at[2 * c + 1]),
        ):
            one.start()
            copies.append(one)
    for one in copies:
        one.wait()


def back(pieces, bits, basis, wt, rights, merged, *kept):
    din, cols = wt.shape
    count = len(pieces)
    width = rights[0].shape[1]
    first = 2 + 2 * count
    return pl.pallas_call(
        functools.partial(back_kernel, pieces, bits),
        out_shape=[
            jax.ShapeDtypeStruct((din, cols), F32),
            jax.ShapeDtypeStruct((1, din, cols), F32),
        ],
        in_specs=[VMEM] * first + [ANY] * len(kept),
        out_specs=[ANY] * 2,
        input_output_aliases={first + n: n for n in range(len(kept))},
        scratch_shapes=[
            pltpu.VMEM((count, din, width), F32),
            pltpu.VMEM((count, din, width), F32),
            pltpu.SemaphoreType.DMA((2 * count,)),
        ],
        compiler_params=pltpu.CompilerParams(vmem_limit_bytes=16 << 20),
    )(basis, wt, *rights, *merged, *kept)


def step(acts, out_grad, weight, error, start_q):
    replicas = lax.axis_size("dp")
    n_tensor = lax.axis_size("tensor")
    bits = [1 << b for b in range(1, replicas.bit_length() - 1)]
    pair = swap(1, 1, replicas)

    rounds = rounds_of(n_tensor)
    tables = [table for table, _ in rounds]
    acts_t, halves, first, rows = first_of(
        acts, out_grad, weight, [tables[0], {}, *tables[1:]]
    )

    def across(block, n):
        return lax.ppermute(block, "tensor", [(a, to) for a, (to, _) in tables[n].items()])

    received = [across(first, 0)]
    theirs, mine = merged_of(acts_t, error, rows)
    came = lax.ppermute(theirs, "dp", pair)
    left = left_of(start_q.T, theirs, mine)
    total, give = begin(mine, came, bits)
    came = lax.ppermute(give, "dp", swap(bits[0], bits[-1], replicas))
    left = left + lax.ppermute(left, "dp", swap(bits[-1], bits[0], replicas))
    for n, (one, other) in enumerate(zip(bits[1:], bits[-2::-1]), 2):
        total = total + came
        came = lax.ppermute(total, "dp", swap(one, other, replicas))
        left = left + lax.ppermute(left, "dp", swap(other, one, replicas))
    left_came = lax.ppermute(left, "dp", pair)

    blocks = rest_of(halves, rows[1:])
    for n in range(1, n_tensor - 1):
        block, adds = blocks[n], rounds[n][1]
        if adds is not None:
            block = summed(block, received[adds])
        received.append(across(block, n))
    relayed = {adds for _, adds in rounds}
    final = [one for n, one in enumerate(received) if n not in relayed]
    input_grad = summed(blocks[0], *final)

    basis = solve(left, left_came, replicas)
    right = right_of(left, left_came, total, came, replicas)
    beside = lax.ppermute(right, "dp", swap(bits[0], bits[-1], replicas))
    diagonal = lax.ppermute(right, "dp", swap(bits[0] | 1, bits[-1] | 1, replicas))
    across_pair = lax.ppermute(right, "dp", pair)
    pieces = ((True, True), (True, False), (False, True))
    rights = (right, beside, across_pair)
    kept = back(pieces, bits, basis, weight, rights, (mine, mine, theirs))
    new_weight, new_error = back(
        ((False, False),), bits, basis, weight, (diagonal,), (theirs,), *kept
    )
    return (new_weight, new_error, input_grad)


def solution(mesh):
    placed = (
        P("dp", None),
        P("dp", "tensor"),
        P(None, "tensor"),
        P("dp", None, "tensor"),
        P("tensor", None),
    )
    return jax.shard_map(
        step,
        mesh=mesh,
        in_specs=placed,
        out_specs=(P(None, "tensor"), P("dp", None, "tensor"), P(("dp", "tensor"), None)),
        check_vma=False,
    )
```

```python
import functools
import math

import jax
import jax.numpy as jnp
from jax import lax
from jax.experimental import pallas as pl
from jax.experimental.pallas import tpu as pltpu
from jax.sharding import PartitionSpec as P


F32 = jnp.float32
BF16 = jnp.bfloat16
NN = (((1,), (0,)), ((), ()))
NT = (((1,), (1,)), ((), ()))
VMEM_BYTES = 67043328
SPARE = 28 << 19
VMEM = pl.BlockSpec(memory_space=pltpu.VMEM)
ANY = pl.BlockSpec(memory_space=pl.ANY)
HBM = pl.BlockSpec(memory_space=pltpu.HBM)


def swap(bit_even, bit_odd, size):
    return [(i, i ^ (bit_odd if i & 1 else bit_even)) for i in range(size)]


def split(x):
    high = x.astype(BF16)
    return high, (x - high.astype(F32)).astype(BF16)


def dot(a, b, dims):
    return lax.dot_general(a, b, dims, preferred_element_type=F32)


def dot3(a, b, dims):
    (ah, al), (bh, bl) = split(a), split(b)
    return dot(ah, bh, dims) + (dot(ah, bl, dims) + dot(al, bh, dims))


def rounds_of(n):
    if n % 2:
        return [({a: ((a + k) % n,) * 2 for a in range(n)}, None) for k in range(1, n)]
    pairs = n // 2

    def member(a, k, parity):
        return 2 * ((a // 2 + k) % pairs) + parity

    give = [
        ({a: (a ^ 1, member(a, k, 1 - a % 2)) for a in range(n)}, None) for k in range(1, pairs)
    ]
    onward = [
        ({a: (member(a, k, a % 2),) * 2 for a in range(n)}, k - 1) for k in range(1, pairs)
    ]
    return [*give, *onward, ({a: (a ^ 1, a ^ 1) for a in range(n)}, None)]


def pick(me, table, n):
    index = jnp.int32(0)
    for a in range(n):
        index = jnp.where(me == a, table[a][1] if table else a, index)
    return index


def part_of(rows, high, low):
    both = jnp.concatenate([high[...], low[...]], axis=1)
    return dot(jnp.concatenate([rows, rows], axis=1), both, NT)


def first_kernel(tables, n, chunks, acts, og, wt, acts_t, high_v, low_v, out, *rest):
    rows_v, (acts_v, wt_v, sems) = rest[:n], rest[n:]
    tok = acts.shape[0]
    _, cols = wt.shape
    block = tok // n
    width = cols // chunks
    me = lax.axis_index("tensor")
    places = [pl.multiple_of(pick(me, table, n) * block, block) for table in tables]

    def load(src, dst, at):
        copy = pltpu.make_async_copy(src, dst, sems.at[at])
        copy.start()
        return copy

    acts_in = [
        load(acts.at[pl.ds(at, block), :], acts_v.at[k * block : (k + 1) * block, :], k)
        for k, at in enumerate(places)
    ]
    wt_in = [
        load(wt.at[:, c * width : (c + 1) * width], wt_v.at[c], 2 * n + c) for c in range(chunks)
    ]
    rows_in = [load(og.at[pl.ds(at, block), :], rows_v[k], n + k) for k, at in enumerate(places)]
    for copy in acts_in:
        copy.wait()
    acts_t[...] = acts_v[...].T
    for c in range(chunks):
        wt_in[c].wait()
        high, low = split(wt_v[c])
        high_v[:, c * width : (c + 1) * width] = high
        low_v[:, c * width : (c + 1) * width] = low
    rows_in[0].wait()
    out[...] = part_of(rows_v[0][...], high_v, low_v)
    for copy in rows_in[1:]:
        copy.wait()


def first_of(acts, og, wt, tables):
    n = len(tables)
    tok = og.shape[0]
    din, cols = wt.shape
    chunks = 2
    block = tok // n
    shape = jax.ShapeDtypeStruct
    acts_t, high, low, out, *rows = pl.pallas_call(
        functools.partial(first_kernel, tables, n, chunks),
        out_shape=[
            shape((din, tok), BF16),
            shape((din, cols), BF16),
            shape((din, cols), BF16),
            shape((block, din), F32),
        ]
        + [shape((block, cols), BF16)] * n,
        in_specs=[HBM] * 3,
        out_specs=[VMEM] * (4 + n),
        scratch_shapes=[
            pltpu.VMEM((tok, din), BF16),
            pltpu.VMEM((chunks, din, cols // chunks), F32),
            pltpu.SemaphoreType.DMA((2 * n + chunks,)),
        ],
        compiler_params=pltpu.CompilerParams(vmem_limit_bytes=VMEM_BYTES - SPARE),
        cost_estimate=pl.CostEstimate(
            flops=4 * block * din * cols, bytes_accessed=4 << 20, transcendentals=0
        ),
        name="first",
    )(acts, og, wt)
    return acts_t, (high, low), out, rows


def rest_kernel(high, low, *rest):
    count = len(rest) // 2
    for rows, out in zip(rest[:count], rest[count:]):
        out[...] = part_of(rows[...], high, low)


def rest_of(halves, rows):
    block, cols = rows[0].shape
    din = halves[0].shape[0]
    return pl.pallas_call(
        rest_kernel,
        out_shape=[jax.ShapeDtypeStruct((block, din), F32)] * len(rows),
        in_specs=[VMEM] * (2 + len(rows)),
        out_specs=[VMEM] * len(rows),
        compiler_params=pltpu.CompilerParams(vmem_limit_bytes=12 << 20),
        cost_estimate=pl.CostEstimate(
            flops=4 * len(rows) * block * din * cols, bytes_accessed=4 << 20, transcendentals=0
        ),
        name="rest",
    )(*halves, *rows)


def merged_kernel(acts_t, err, *rest):
    rows, (theirs, mine) = rest[:-2], rest[-2:]
    tok = acts_t.shape[1]
    half = theirs.shape[1]
    side = lax.rem(lax.axis_index("dp"), 2)
    scale = 1.0 / math.sqrt(tok)
    for where, out in ((1 - side, theirs), (side, mine)):
        span = pl.ds(pl.multiple_of(where * half, half), half)
        columns = jnp.concatenate([one[:, span] for one in rows], axis=0)
        out[...] = dot(acts_t[...], columns, NN) * scale + err[0, :, span]


def merged_of(acts_t, err, rows):
    din, cols = err.shape[1:]
    tok = acts_t.shape[1]
    return pl.pallas_call(
        merged_kernel,
        out_shape=[jax.ShapeDtypeStruct((din, cols // 2), F32)] * 2,
        in_specs=[VMEM] * (2 + len(rows)),
        out_specs=[VMEM] * 2,
        compiler_params=pltpu.CompilerParams(vmem_limit_bytes=8 << 20),
        cost_estimate=pl.CostEstimate(
            flops=2 * tok * din * cols, bytes_accessed=4 << 20, transcendentals=0
        ),
        name="merged",
    )(acts_t, err, *rows)


def sum_kernel(*refs):
    total = refs[0][...]
    for part in refs[1:-1]:
        total = total + part[...]
    refs[-1][...] = total


def summed(*parts):
    return pl.pallas_call(
        sum_kernel,
        out_shape=jax.ShapeDtypeStruct(parts[0].shape, F32),
        in_specs=[VMEM] * len(parts),
        out_specs=VMEM,
        compiler_params=pltpu.CompilerParams(vmem_limit_bytes=4 << 20),
    )(*parts)


def left_kernel(qt, theirs, mine, o_ref):
    half = theirs.shape[1]
    side = lax.rem(lax.axis_index("dp"), 2)
    far = qt[:, pl.ds(pl.multiple_of((1 - side) * half, half), half)]
    near = qt[:, pl.ds(pl.multiple_of(side * half, half), half)]
    o_ref[...] = dot3(far, theirs[...], NT) + dot3(near, mine[...], NT)


def left_of(qt, theirs, mine):
    return pl.pallas_call(
        left_kernel,
        out_shape=jax.ShapeDtypeStruct((qt.shape[0], mine.shape[0]), F32),
        in_specs=[VMEM] * 3,
        out_specs=VMEM,
        compiler_params=pltpu.CompilerParams(vmem_limit_bytes=8 << 20),
        name="left",
    )(qt, theirs, mine)


def solve_kernel(replicas, a_ref, b_ref, y_ref):
    left = (a_ref[...] + b_ref[...]) * (1.0 / replicas)
    rank, din = left.shape
    gram = lax.dot_general(
        left, left, NT, precision=lax.Precision.HIGHEST, preferred_element_type=F32
    )
    tiles, lanes = rank // 8, 128
    spans = range(0, din, lanes)
    state = [
        [gram[8 * i : 8 * i + 8, :]] + [left[8 * i : 8 * i + 8, at : at + lanes] for at in spans]
        for i in range(tiles)
    ]
    sub = lax.broadcasted_iota(jnp.int32, (8, lanes), 0)
    for k in range(0, rank, 2):
        i, s = divmod(k, 8)
        first = [jnp.broadcast_to(row[0][:, k : k + 1], (8, lanes)) for row in state]
        second = [jnp.broadcast_to(row[0][:, k + 1 : k + 2], (8, lanes)) for row in state]
        a = first[i][s : s + 1, :]
        b = second[i][s : s + 1, :]
        d = second[i][s + 1 : s + 2, :]
        inverse = 1.0 / (a * d - b * b)
        p, q, r = d * inverse, b * inverse, a * inverse
        for part in range(len(state[0])):
            wide = state[0][part].shape[1]
            top = state[i][part][s : s + 1, :]
            low = state[i][part][s + 1 : s + 2, :]
            new_top = p[:, :wide] * top - q[:, :wide] * low
            new_low = r[:, :wide] * low - q[:, :wide] * top
            for j in range(tiles):
                old = state[j][part]
                new = old - first[j][:, :wide] * new_top - second[j][:, :wide] * new_low
                if j == i:
                    new = jnp.where(sub[:, :wide] == s, new_top, new)
                    new = jnp.where(sub[:, :wide] == s + 1, new_low, new)
                state[j][part] = new
    for j in range(tiles):
        for n, at in enumerate(spans):
            y_ref[8 * j : 8 * j + 8, at : at + lanes] = state[j][1 + n]


def solve(a, b, replicas):
    return pl.pallas_call(
        functools.partial(solve_kernel, replicas),
        out_shape=jax.ShapeDtypeStruct(a.shape, F32),
        in_specs=[VMEM] * 2,
        out_specs=VMEM,
        compiler_params=pltpu.CompilerParams(vmem_limit_bytes=4 << 20),
        cost_estimate=pl.CostEstimate(
            flops=1 << 30, bytes_accessed=1 << 20, transcendentals=0
        ),
        name="solve",
    )(a, b)


def quarter(bits, side, index):
    even, odd = (lax.rem(index // bit, 2) for bit in (bits[0], bits[-1]))
    return jnp.where(side == 0, even, odd)


def begin_kernel(bits, mine, came, keep, give):
    width = keep.shape[1]
    index = lax.axis_index("dp")
    own = quarter(bits, lax.rem(index, 2), index)
    for which, out in ((own, keep), (1 - own, give)):
        span = pl.ds(pl.multiple_of(which * width, width), width)
        out[...] = mine[:, span] + came[:, span]


def begin(mine, came, bits):
    din, half = mine.shape
    return pl.pallas_call(
        functools.partial(begin_kernel, bits),
        out_shape=[jax.ShapeDtypeStruct((din, half // 2), F32)] * 2,
        in_specs=[VMEM] * 2,
        out_specs=[VMEM] * 2,
        compiler_params=pltpu.CompilerParams(vmem_limit_bytes=4 << 20),
        name="begin",
    )(mine, came)


def right_kernel(replicas, left_a, left_b, total_a, total_b, out):
    left = (left_a[...] + left_b[...]) * (1.0 / replicas)
    out[...] = dot3(left, (total_a[...] + total_b[...]) * (1.0 / replicas), NN)


def right_of(left, left_came, total, came, replicas):
    return pl.pallas_call(
        functools.partial(right_kernel, replicas),
        out_shape=jax.ShapeDtypeStruct((left.shape[0], total.shape[1]), F32),
        in_specs=[VMEM] * 4,
        out_specs=VMEM,
        compiler_params=pltpu.CompilerParams(vmem_limit_bytes=8 << 20),
        name="right",
    )(left, left_came, total, came)


def back_kernel(pieces, bits, basis, wt, *rest):
    count = len(pieces)
    rights, merged = rest[:count], rest[count : 2 * count]
    new_w, new_e, wv, ev, sems = rest[-5:]
    width = rights[0].shape[1]
    index = lax.axis_index("dp")
    flipped = basis[...].T
    copies = []
    for c, (near, same) in enumerate(pieces):
        side = lax.rem(index, 2)
        side = side if near else 1 - side
        own = quarter(bits, side, index)
        which = own if same else 1 - own
        here = pl.ds(pl.multiple_of(which * width, width), width)
        span = pl.ds(pl.multiple_of((2 * side + which) * width, width), width)
        delta = dot3(flipped, rights[c][...], NN)
        ev[c] = merged[c][:, here] - delta
        wv[c] = wt[:, span] - delta
        for one in (
            pltpu.make_async_copy(ev.at[c], new_e.at[0, :, span], sems.at[2 * c]),
            pltpu.make_async_copy(wv.at[c], new_w.at[:, span], sems.at[2 * c + 1]),
        ):
            one.start()
            copies.append(one)
    for one in copies:
        one.wait()


def back(pieces, bits, basis, wt, rights, merged, *kept):
    din, cols = wt.shape
    count = len(pieces)
    width = rights[0].shape[1]
    first = 2 + 2 * count
    return pl.pallas_call(
        functools.partial(back_kernel, pieces, bits),
        out_shape=[
            jax.ShapeDtypeStruct((din, cols), F32),
            jax.ShapeDtypeStruct((1, din, cols), F32),
        ],
        in_specs=[VMEM] * first + [ANY] * len(kept),
        out_specs=[ANY] * 2,
        input_output_aliases={first + n: n for n in range(len(kept))},
        scratch_shapes=[
            pltpu.VMEM((count, din, width), F32),
            pltpu.VMEM((count, din, width), F32),
            pltpu.SemaphoreType.DMA((2 * count,)),
        ],
        compiler_params=pltpu.CompilerParams(vmem_limit_bytes=16 << 20),
    )(basis, wt, *rights, *merged, *kept)


def step(acts, out_grad, weight, error, start_q):
    replicas = lax.axis_size("dp")
    n_tensor = lax.axis_size("tensor")
    bits = [1 << b for b in range(1, replicas.bit_length() - 1)]
    pair = swap(1, 1, replicas)

    rounds = rounds_of(n_tensor)
    tables = [table for table, _ in rounds]
    acts_t, halves, first, rows = first_of(
        acts, out_grad, weight, [tables[0], {}, *tables[1:]]
    )

    def across(block, n):
        return lax.ppermute(block, "tensor", [(a, to) for a, (to, _) in tables[n].items()])

    received = [across(first, 0)]
    theirs, mine = merged_of(acts_t, error, rows)
    came = lax.ppermute(theirs, "dp", pair)
    left = left_of(start_q.T, theirs, mine)
    total, give = begin(mine, came, bits)
    came = lax.ppermute(give, "dp", swap(bits[0], bits[-1], replicas))
    left = left + lax.ppermute(left, "dp", swap(bits[-1], bits[0], replicas))
    for n, (one, other) in enumerate(zip(bits[1:], bits[-2::-1]), 2):
        total = total + came
        came = lax.ppermute(total, "dp", swap(one, other, replicas))
        left = left + lax.ppermute(left, "dp", swap(other, one, replicas))
    left_came = lax.ppermute(left, "dp", pair)

    blocks = rest_of(halves, rows[1:])
    for n in range(1, n_tensor - 1):
        block, adds = blocks[n], rounds[n][1]
        if adds is not None:
            block = summed(block, received[adds])
        received.append(across(block, n))
    relayed = {adds for _, adds in rounds}
    final = [one for n, one in enumerate(received) if n not in relayed]
    input_grad = summed(blocks[0], *final)

    basis = solve(left, left_came, replicas)
    right = right_of(left, left_came, total, came, replicas)
    across_pair = lax.ppermute(right, "dp", pair)
    beside = lax.ppermute(right, "dp", swap(bits[0], bits[-1], replicas))
    diagonal = lax.ppermute(right, "dp", swap(bits[0] | 1, bits[-1] | 1, replicas))
    merged = (mine, theirs)
    pieces, rights = ((True, True), (False, True)), (right, across_pair)
    kept = back(pieces, bits, basis, weight, rights, merged)
    pieces, rights = ((True, False), (False, False)), (beside, diagonal)
    new_weight, new_error = back(pieces, bits, basis, weight, rights, merged, *kept)
    return (new_weight, new_error, input_grad)


def solution(mesh):
    placed = (
        P("dp", None),
        P("dp", "tensor"),
        P(None, "tensor"),
        P("dp", None, "tensor"),
        P("tensor", None),
    )
    return jax.shard_map(
        step,
        mesh=mesh,
        in_specs=placed,
        out_specs=(P(None, "tensor"), P("dp", None, "tensor"), P(("dp", "tensor"), None)),
        check_vma=False,
    )
```

```python
import functools
import math

import jax
import jax.numpy as jnp
from jax import lax
from jax.experimental import pallas as pl
from jax.experimental.pallas import tpu as pltpu
from jax.sharding import PartitionSpec as P


F32 = jnp.float32
BF16 = jnp.bfloat16
NN = (((1,), (0,)), ((), ()))
NT = (((1,), (1,)), ((), ()))
VMEM_BYTES = 67043328
SPARE = 28 << 19
VMEM = pl.BlockSpec(memory_space=pltpu.VMEM)
ANY = pl.BlockSpec(memory_space=pl.ANY)
HBM = pl.BlockSpec(memory_space=pltpu.HBM)


def swap(bit_even, bit_odd, size):
    return [(i, i ^ (bit_odd if i & 1 else bit_even)) for i in range(size)]


def split(x):
    high = x.astype(BF16)
    return high, (x - high.astype(F32)).astype(BF16)


def dot(a, b, dims):
    return lax.dot_general(a, b, dims, preferred_element_type=F32)


def dot3(a, b, dims):
    (ah, al), (bh, bl) = split(a), split(b)
    return dot(ah, bh, dims) + (dot(ah, bl, dims) + dot(al, bh, dims))


def rounds_of(n):
    if n % 2:
        return [({a: ((a + k) % n,) * 2 for a in range(n)}, None) for k in range(1, n)]
    pairs = n // 2

    def member(a, k, parity):
        return 2 * ((a // 2 + k) % pairs) + parity

    give = [
        ({a: (a ^ 1, member(a, k, 1 - a % 2)) for a in range(n)}, None) for k in range(1, pairs)
    ]
    onward = [
        ({a: (member(a, k, a % 2),) * 2 for a in range(n)}, k - 1) for k in range(1, pairs)
    ]
    return [*give, *onward, ({a: (a ^ 1, a ^ 1) for a in range(n)}, None)]


def pick(me, table, n):
    index = jnp.int32(0)
    for a in range(n):
        index = jnp.where(me == a, table[a][1] if table else a, index)
    return index


def part_of(rows, high, low):
    both = jnp.concatenate([high[...], low[...]], axis=1)
    return dot(jnp.concatenate([rows, rows], axis=1), both, NT)


def first_kernel(tables, n, chunks, acts, og, wt, acts_t, high_v, low_v, out, *rest):
    rows_v, (acts_v, wt_v, sems) = rest[:n], rest[n:]
    tok = acts.shape[0]
    _, cols = wt.shape
    block = tok // n
    width = cols // chunks
    me = lax.axis_index("tensor")
    places = [pl.multiple_of(pick(me, table, n) * block, block) for table in tables]

    def load(src, dst, at):
        copy = pltpu.make_async_copy(src, dst, sems.at[at])
        copy.start()
        return copy

    acts_in = [
        load(acts.at[pl.ds(at, block), :], acts_v.at[k * block : (k + 1) * block, :], k)
        for k, at in enumerate(places)
    ]
    wt_in = [
        load(wt.at[:, c * width : (c + 1) * width], wt_v.at[c], 2 * n + c) for c in range(chunks)
    ]
    rows_in = [load(og.at[pl.ds(at, block), :], rows_v[k], n + k) for k, at in enumerate(places)]
    for copy in acts_in:
        copy.wait()
    acts_t[...] = acts_v[...].T
    for c in range(chunks):
        wt_in[c].wait()
        high, low = split(wt_v[c])
        high_v[:, c * width : (c + 1) * width] = high
        low_v[:, c * width : (c + 1) * width] = low
    rows_in[0].wait()
    out[...] = part_of(rows_v[0][...], high_v, low_v)
    for copy in rows_in[1:]:
        copy.wait()


def first_of(acts, og, wt, tables):
    n = len(tables)
    tok = og.shape[0]
    din, cols = wt.shape
    chunks = 2
    block = tok // n
    shape = jax.ShapeDtypeStruct
    acts_t, high, low, out, *rows = pl.pallas_call(
        functools.partial(first_kernel, tables, n, chunks),
        out_shape=[
            shape((din, tok), BF16),
            shape((din, cols), BF16),
            shape((din, cols), BF16),
            shape((block, din), F32),
        ]
        + [shape((block, cols), BF16)] * n,
        in_specs=[HBM] * 3,
        out_specs=[VMEM] * (4 + n),
        scratch_shapes=[
            pltpu.VMEM((tok, din), BF16),
            pltpu.VMEM((chunks, din, cols // chunks), F32),
            pltpu.SemaphoreType.DMA((2 * n + chunks,)),
        ],
        compiler_params=pltpu.CompilerParams(vmem_limit_bytes=VMEM_BYTES - SPARE),
        cost_estimate=pl.CostEstimate(
            flops=4 * block * din * cols, bytes_accessed=4 << 20, transcendentals=0
        ),
        name="first",
    )(acts, og, wt)
    return acts_t, (high, low), out, rows


def rest_kernel(high, low, *rest):
    count = len(rest) // 2
    for rows, out in zip(rest[:count], rest[count:]):
        out[...] = part_of(rows[...], high, low)


def rest_of(halves, rows):
    block, cols = rows[0].shape
    din = halves[0].shape[0]
    return pl.pallas_call(
        rest_kernel,
        out_shape=[jax.ShapeDtypeStruct((block, din), F32)] * len(rows),
        in_specs=[VMEM] * (2 + len(rows)),
        out_specs=[VMEM] * len(rows),
        compiler_params=pltpu.CompilerParams(vmem_limit_bytes=12 << 20),
        cost_estimate=pl.CostEstimate(
            flops=4 * len(rows) * block * din * cols, bytes_accessed=4 << 20, transcendentals=0
        ),
    )(*halves, *rows)


def merged_kernel(acts_t, err, *rest):
    rows, (theirs, mine) = rest[:-2], rest[-2:]
    tok = acts_t.shape[1]
    half = theirs.shape[1]
    side = lax.rem(lax.axis_index("dp"), 2)
    scale = 1.0 / math.sqrt(tok)
    for where, out in ((1 - side, theirs), (side, mine)):
        span = pl.ds(pl.multiple_of(where * half, half), half)
        columns = jnp.concatenate([one[:, span] for one in rows], axis=0)
        out[...] = dot(acts_t[...], columns, NN) * scale + err[0, :, span]


def merged_of(acts_t, err, rows):
    din, cols = err.shape[1:]
    tok = acts_t.shape[1]
    return pl.pallas_call(
        merged_kernel,
        out_shape=[jax.ShapeDtypeStruct((din, cols // 2), F32)] * 2,
        in_specs=[VMEM] * (2 + len(rows)),
        out_specs=[VMEM] * 2,
        compiler_params=pltpu.CompilerParams(vmem_limit_bytes=8 << 20),
        cost_estimate=pl.CostEstimate(
            flops=2 * tok * din * cols, bytes_accessed=4 << 20, transcendentals=0
        ),
        name="merged",
    )(acts_t, err, *rows)


def sum_kernel(*refs):
    total = refs[0][...]
    for part in refs[1:-1]:
        total = total + part[...]
    refs[-1][...] = total


def summed(*parts):
    return pl.pallas_call(
        sum_kernel,
        out_shape=jax.ShapeDtypeStruct(parts[0].shape, F32),
        in_specs=[VMEM] * len(parts),
        out_specs=VMEM,
        compiler_params=pltpu.CompilerParams(vmem_limit_bytes=4 << 20),
    )(*parts)


def left_kernel(qt, theirs, mine, o_ref):
    half = theirs.shape[1]
    side = lax.rem(lax.axis_index("dp"), 2)
    far = qt[:, pl.ds(pl.multiple_of((1 - side) * half, half), half)]
    near = qt[:, pl.ds(pl.multiple_of(side * half, half), half)]
    o_ref[...] = dot3(far, theirs[...], NT) + dot3(near, mine[...], NT)


def left_of(qt, theirs, mine):
    return pl.pallas_call(
        left_kernel,
        out_shape=jax.ShapeDtypeStruct((qt.shape[0], mine.shape[0]), F32),
        in_specs=[VMEM] * 3,
        out_specs=VMEM,
        compiler_params=pltpu.CompilerParams(vmem_limit_bytes=8 << 20),
        name="left",
    )(qt, theirs, mine)


def solve_kernel(replicas, a_ref, b_ref, y_ref):
    left = (a_ref[...] + b_ref[...]) * (1.0 / replicas)
    rank, din = left.shape
    gram = lax.dot_general(
        left, left, NT, precision=lax.Precision.HIGHEST, preferred_element_type=F32
    )
    tiles, lanes = rank // 8, 128
    spans = range(0, din, lanes)
    state = [
        [gram[8 * i : 8 * i + 8, :]] + [left[8 * i : 8 * i + 8, at : at + lanes] for at in spans]
        for i in range(tiles)
    ]
    sub = lax.broadcasted_iota(jnp.int32, (8, lanes), 0)
    for k in range(0, rank, 2):
        i, s = divmod(k, 8)
        first = [jnp.broadcast_to(row[0][:, k : k + 1], (8, lanes)) for row in state]
        second = [jnp.broadcast_to(row[0][:, k + 1 : k + 2], (8, lanes)) for row in state]
        a = first[i][s : s + 1, :]
        b = second[i][s : s + 1, :]
        d = second[i][s + 1 : s + 2, :]
        inverse = 1.0 / (a * d - b * b)
        p, q, r = d * inverse, b * inverse, a * inverse
        for part in range(len(state[0])):
            wide = state[0][part].shape[1]
            top = state[i][part][s : s + 1, :]
            low = state[i][part][s + 1 : s + 2, :]
            new_top = p[:, :wide] * top - q[:, :wide] * low
            new_low = r[:, :wide] * low - q[:, :wide] * top
            for j in range(tiles):
                old = state[j][part]
                new = old - first[j][:, :wide] * new_top - second[j][:, :wide] * new_low
                if j == i:
                    new = jnp.where(sub[:, :wide] == s, new_top, new)
                    new = jnp.where(sub[:, :wide] == s + 1, new_low, new)
                state[j][part] = new
    for j in range(tiles):
        for n, at in enumerate(spans):
            y_ref[8 * j : 8 * j + 8, at : at + lanes] = state[j][1 + n]


def solve(a, b, replicas):
    return pl.pallas_call(
        functools.partial(solve_kernel, replicas),
        out_shape=jax.ShapeDtypeStruct(a.shape, F32),
        in_specs=[VMEM] * 2,
        out_specs=VMEM,
        compiler_params=pltpu.CompilerParams(vmem_limit_bytes=4 << 20),
        cost_estimate=pl.CostEstimate(
            flops=1 << 30, bytes_accessed=1 << 20, transcendentals=0
        ),
        name="solve",
    )(a, b)


def quarter(bits, side, index):
    even, odd = (lax.rem(index // bit, 2) for bit in (bits[0], bits[-1]))
    return jnp.where(side == 0, even, odd)


def begin_kernel(bits, mine, came, keep, give):
    width = keep.shape[1]
    index = lax.axis_index("dp")
    own = quarter(bits, lax.rem(index, 2), index)
    for which, out in ((own, keep), (1 - own, give)):
        span = pl.ds(pl.multiple_of(which * width, width), width)
        out[...] = mine[:, span] + came[:, span]


def begin(mine, came, bits):
    din, half = mine.shape
    return pl.pallas_call(
        functools.partial(begin_kernel, bits),
        out_shape=[jax.ShapeDtypeStruct((din, half // 2), F32)] * 2,
        in_specs=[VMEM] * 2,
        out_specs=[VMEM] * 2,
        compiler_params=pltpu.CompilerParams(vmem_limit_bytes=4 << 20),
        name="begin",
    )(mine, came)


def right_kernel(replicas, left_a, left_b, total_a, total_b, out):
    left = (left_a[...] + left_b[...]) * (1.0 / replicas)
    out[...] = dot3(left, (total_a[...] + total_b[...]) * (1.0 / replicas), NN)


def right_of(left, left_came, total, came, replicas):
    return pl.pallas_call(
        functools.partial(right_kernel, replicas),
        out_shape=jax.ShapeDtypeStruct((left.shape[0], total.shape[1]), F32),
        in_specs=[VMEM] * 4,
        out_specs=VMEM,
        compiler_params=pltpu.CompilerParams(vmem_limit_bytes=8 << 20),
        name="right",
    )(left, left_came, total, came)


def back_kernel(pieces, bits, basis, wt, *rest):
    count = len(pieces)
    rights, merged = rest[:count], rest[count : 2 * count]
    new_w, new_e, wv, ev, sems = rest[-5:]
    width = rights[0].shape[1]
    index = lax.axis_index("dp")
    flipped = basis[...].T
    copies = []
    for c, (near, same) in enumerate(pieces):
        side = lax.rem(index, 2)
        side = side if near else 1 - side
        own = quarter(bits, side, index)
        which = own if same else 1 - own
        here = pl.ds(pl.multiple_of(which * width, width), width)
        span = pl.ds(pl.multiple_of((2 * side + which) * width, width), width)
        delta = dot3(flipped, rights[c][...], NN)
        ev[c] = merged[c][:, here] - delta
        wv[c] = wt[:, span] - delta
        for one in (
            pltpu.make_async_copy(ev.at[c], new_e.at[0, :, span], sems.at[2 * c]),
            pltpu.make_async_copy(wv.at[c], new_w.at[:, span], sems.at[2 * c + 1]),
        ):
            one.start()
            copies.append(one)
    for one in copies:
        one.wait()


def back(pieces, bits, basis, wt, rights, merged, *kept):
    din, cols = wt.shape
    count = len(pieces)
    width = rights[0].shape[1]
    first = 2 + 2 * count
    return pl.pallas_call(
        functools.partial(back_kernel, pieces, bits),
        out_shape=[
            jax.ShapeDtypeStruct((din, cols), F32),
            jax.ShapeDtypeStruct((1, din, cols), F32),
        ],
        in_specs=[VMEM] * first + [ANY] * len(kept),
        out_specs=[ANY] * 2,
        input_output_aliases={first + n: n for n in range(len(kept))},
        scratch_shapes=[
            pltpu.VMEM((count, din, width), F32),
            pltpu.VMEM((count, din, width), F32),
            pltpu.SemaphoreType.DMA((2 * count,)),
        ],
        compiler_params=pltpu.CompilerParams(vmem_limit_bytes=16 << 20),
    )(basis, wt, *rights, *merged, *kept)


def step(acts, out_grad, weight, error, start_q):
    replicas = lax.axis_size("dp")
    n_tensor = lax.axis_size("tensor")
    bits = [1 << b for b in range(1, replicas.bit_length() - 1)]
    pair = swap(1, 1, replicas)

    rounds = rounds_of(n_tensor)
    tables = [table for table, _ in rounds]
    acts_t, halves, first, rows = first_of(
        acts, out_grad, weight, [tables[0], {}, *tables[1:]]
    )

    def across(block, n):
        return lax.ppermute(block, "tensor", [(a, to) for a, (to, _) in tables[n].items()])

    received = [across(first, 0)]
    theirs, mine = merged_of(acts_t, error, rows)
    came = lax.ppermute(theirs, "dp", pair)
    left = left_of(start_q.T, theirs, mine)
    total, give = begin(mine, came, bits)
    came = lax.ppermute(give, "dp", swap(bits[0], bits[-1], replicas))
    left = left + lax.ppermute(left, "dp", swap(bits[-1], bits[0], replicas))
    for n, (one, other) in enumerate(zip(bits[1:], bits[-2::-1]), 2):
        total = total + came
        came = lax.ppermute(total, "dp", swap(one, other, replicas))
        left = left + lax.ppermute(left, "dp", swap(other, one, replicas))
    left_came = lax.ppermute(left, "dp", pair)

    blocks = rest_of(halves, rows[2:])
    for n in range(1, n_tensor - 1):
        block, adds = blocks[n - 1], rounds[n][1]
        if adds is not None:
            block = summed(block, received[adds])
        received.append(across(block, n))
    relayed = {adds for _, adds in rounds}
    final = [one for n, one in enumerate(received) if n not in relayed]
    own = rest_of(halves, rows[1:2])[0]
    input_grad = summed(own, *final)

    basis = solve(left, left_came, replicas)
    right = right_of(left, left_came, total, came, replicas)
    across_pair = lax.ppermute(right, "dp", pair)
    beside = lax.ppermute(right, "dp", swap(bits[0], bits[-1], replicas))
    diagonal = lax.ppermute(right, "dp", swap(bits[0] | 1, bits[-1] | 1, replicas))
    merged = (mine, theirs)
    pieces, rights = ((True, True), (False, True)), (right, across_pair)
    kept = back(pieces, bits, basis, weight, rights, merged)
    pieces, rights = ((True, False), (False, False)), (beside, diagonal)
    new_weight, new_error = back(pieces, bits, basis, weight, rights, merged, *kept)
    return (new_weight, new_error, input_grad)


def solution(mesh):
    placed = (
        P("dp", None),
        P("dp", "tensor"),
        P(None, "tensor"),
        P("dp", None, "tensor"),
        P("tensor", None),
    )
    return jax.shard_map(
        step,
        mesh=mesh,
        in_specs=placed,
        out_specs=(P(None, "tensor"), P("dp", None, "tensor"), P(("dp", "tensor"), None)),
        check_vma=False,
    )
```
